512 devices in a mesh: tm: 32 (over z, core), space: 16 (over x, y).
Axes of the slice: x: 4, y: 4, z: 16, core: 2. Of those that a mesh axis runs over, the one named last changes fastest.
Arguments:
- sections: int32 [32], replicated, may hold values from 1 to 4, 80 in all
- right_side: bfloat16 [128, 64, 2048], P('tm'), may hold values from -6 to 6
- tip_side: float32 [64, 8], replicated, may hold values from -48 to 48
- diag_inverse: bfloat16 [128, 2048, 2048], P('tm', 'space'), may hold values from -0.08 to 0.42, as said below
- forward_coupling: bfloat16 [128, 2048, 128], P('tm', 'space'), may hold values from -1 to 1
- backward_coupling: bfloat16 [128, 2048, 128], P('tm', 'space'), may hold values from -1 to 1
- arrow_rows: bfloat16 [128, 8, 2048], P('tm', None, 'space'), may hold values from -3.3 to 3.3
- tip_inverse: float32 [8, 8], replicated, may hold values from -0.4 to 0.4, as said below
Outputs:
- solution: float32 [128, 64, 2048], P('tm', None, 'space')
- tip_solution: float32 [64, 8], replicated
The draws below stay inside these ranges and needn't reach their ends.
Inputs may be any that keep to these rules, and one draw needn't show every extreme that they name: Section i holds the live slots i * 4 to i * 4 + sections[i] - 1. `diag_inverse`: each block is lower triangular with a positive diagonal. `tip_inverse`: lower triangular with a positive diagonal.
All inputs are finite; a program needn't handle non-finite values.
Results may differ from the reference program's by a relative error of at most 0.0031.
Values sent between devices are 32-bit elements; how exact they have to be, the bound alone decides.
No kernel may reach another device: no remote copies, remote signals or barrier semaphores. Data moves between devices by JAX's collectives and lax.ppermute only.
A program may use at most 64 MiB of HBM per device.

```python
import math
import jax
import jax.numpy as jnp
import numpy as np
from jax import lax

S = 2048
SUB = 128
F = 8
RHS = 64
CAP = 4
SLOTS = 128
TBLK = 80
N_TM = 32


def rough_field(key, shape):
    return jax.random.normal(key, shape, jnp.float32)


def draw_diag_inverse(key, part):
    key_rough = jax.random.fold_in(key, 13)
    key_diag = jax.random.fold_in(key, 31)
    indices = jnp.arange(S)
    below_diag = indices[:, None] > indices[None, :]
    on_diagonal = indices[:, None] == indices[None, :]
    diagonal = jax.random.uniform(key_diag, (SLOTS, S), jnp.float32, 0.6, 1.4)
    slot_keys = jax.random.split(key_rough, SLOTS)

    def one_slot(pair):
        slot_key, diag_row = pair
        rough = jnp.clip(rough_field(slot_key, (S, S)), -4.0, 4.0)
        combined = jnp.where(below_diag, 0.5 * rough / jnp.sqrt(S * 1.0), 0.0) + jnp.where(on_diagonal, diag_row[:, None], 0.0)
        return (0.3 * combined).astype(jnp.bfloat16)
    return lax.map(one_slot, (slot_keys, diagonal))


def draw_forward_coupling(key, part):
    rough = jnp.clip(rough_field(jax.random.fold_in(key, 11), (SLOTS, S, SUB)), -2.0, 2.0)
    return (0.96 * rough / jnp.sqrt(SUB * 1.0)).astype(jnp.bfloat16)


def draw_backward_coupling(key, part):
    rough = jnp.clip(rough_field(jax.random.fold_in(key, 12), (SLOTS, S, SUB)), -2.0, 2.0)
    return (0.96 * rough / jnp.sqrt(SUB * 1.0)).astype(jnp.bfloat16)


def draw_arrow_rows(key, part):
    rough = jnp.clip(rough_field(jax.random.fold_in(key, 14), (SLOTS, F, S)), -4.0, 4.0)
    slot_ramp = 0.6 * 3.0 ** (jnp.arange(SLOTS, dtype=jnp.float32) / (SLOTS - 1))
    row_scale = 32.0 / jnp.sqrt(TBLK * S * 1.0)
    scaled = jnp.clip(row_scale * slot_ramp[:, None, None] * rough, -3.25, 3.25)
    return scaled.astype(jnp.bfloat16)


def draw_tip_inverse(key, part):
    key_rough = jax.random.fold_in(key, 15)
    key_diag = jax.random.fold_in(key, 51)
    indices = jnp.arange(F)
    below_diag = indices[:, None] > indices[None, :]
    on_diagonal = indices[:, None] == indices[None, :]
    rough = jnp.clip(rough_field(key_rough, (F, F)), -4.0, 4.0)
    diagonal = jax.random.uniform(key_diag, (F,), jnp.float32, 0.8, 1.2)
    combined = jnp.where(below_diag, 0.3 * rough, 0.0) + jnp.where(on_diagonal, diagonal[:, None], 0.0)
    return 0.17 * combined


def block_scale(own_key, shape, pieces, least, top_value):
    def one(axis_at, parts):
        heights = jax.random.uniform(jax.random.fold_in(jax.random.fold_in(own_key, 6), axis_at), (parts,), jnp.float32, least / len(pieces), top_value / len(pieces))
        return jnp.repeat(jnp.exp(heights), shape[axis_at] // parts).reshape((-1,) + (1,) * (len(shape) - axis_at - 1))

    level = one(*pieces[0])
    for cut in pieces[1:]:
        level = level * one(*cut)
    return level


def profile(count, total, reach, lean):
    portions = [(1 << 20) // math.isqrt(rank ** lean) + 1 for rank in range(2, count + 1)]
    surplus, holding = total - reach - (count - 1), [1] * (count - 1)
    while surplus > 0:
        candidates = [i for i in range(count - 1) if holding[i] < reach]
        pool, left = sum([portions[i] for i in candidates]), surplus
        for i in candidates:
            addition = min(reach - holding[i], max(1, left * portions[i] // pool), surplus)
            holding[i] = holding[i] + addition
            surplus = surplus - addition
    return np.array([reach] + holding)


def uneven(own_key, count, total, limit, skew):
    if count == 2:
        one = jax.random.randint(own_key, (), max(1, total - limit), min(limit, total - 1) + 1)
        return jnp.stack([one, total - one])
    sizes = jnp.asarray(profile(count, total, limit, skew), jnp.int32)
    twos = (count - 1) // 2
    source_of, taker = sizes[1:1 + 2 * twos:2], sizes[2:2 + 2 * twos:2]
    slack = jnp.minimum(source_of - 1, limit - taker)
    shifted = jax.random.randint(jax.random.fold_in(own_key, 1), (twos,), 0, 1 << 20) % (slack + 1)
    sizes = sizes.at[1:1 + 2 * twos:2].set(source_of - shifted).at[2:2 + 2 * twos:2].set(taker + shifted)
    return sizes[jax.random.permutation(jax.random.fold_in(own_key, 2), count)]


def scatter_about(stream_key, shape, spread, reach, cuts=(), held_as=jnp.bfloat16):
    values = spread * jax.random.normal(stream_key, shape, jnp.float32)
    if cuts:
        values = values * block_scale(stream_key, shape, cuts, -0.22, 0.18)
    return jnp.clip(values, -reach, reach).astype(held_as)


def setup_inputs(seed: int = 0) -> dict:
    key_list = jax.random.split(jax.random.key(seed), 9)
    return {
        "sections": uneven(key_list[0], N_TM, N_TM * 5 // 2, CAP, 2).astype(jnp.int32),
        "right_side": scatter_about(key_list[1], (SLOTS, RHS, S), 1.0, 6.0, ((0, 32),)),
        "tip_side": scatter_about(key_list[2], (RHS, F), 8.0, 48.0, (), jnp.float32),
        "diag_inverse": draw_diag_inverse(jax.random.fold_in(key_list[8], 71), 0),
        "forward_coupling": draw_forward_coupling(jax.random.fold_in(key_list[8], 71), 0),
        "backward_coupling": draw_backward_coupling(jax.random.fold_in(key_list[8], 71), 0),
        "arrow_rows": draw_arrow_rows(jax.random.fold_in(key_list[8], 71), 0),
        "tip_inverse": draw_tip_inverse(jax.random.fold_in(key_list[8], 71), 0),
    }


def couple(states, coupling):
    row_count = states.shape[0]
    sub_count = S // SUB
    shaped = states.reshape(row_count, sub_count, SUB)
    blocks = coupling.astype(jnp.float32).reshape(sub_count, SUB, SUB)
    return jnp.einsum("rnk,nik->rni", shaped, blocks, precision=lax.Precision.HIGHEST).reshape(row_count, S)


def reference(sections, right_side, tip_side, diag_inverse, forward_coupling, backward_coupling, arrow_rows, tip_inverse):
    slot_ids = jnp.arange(SLOTS, dtype=jnp.int32)
    live_slot = (slot_ids % CAP) < jnp.repeat(sections, CAP)

    def forward_step(carried, inputs):
        side_block, inverse_block, coupling_block, live_flag = inputs
        driven = jnp.dot(side_block, inverse_block.T, preferred_element_type=jnp.float32)
        update = driven - couple(carried, coupling_block)
        state = jnp.where(live_flag, update, jnp.float32(0.0))
        carried = jnp.where(live_flag, update, carried)
        return carried, state

    start = jnp.zeros((RHS, S), jnp.float32)
    _, forward_state = lax.scan(forward_step, start, (right_side, diag_inverse, forward_coupling, live_slot))
    arrow_wide = arrow_rows.astype(jnp.float32)
    arrow_total = jnp.einsum("trs,tfs->rf", forward_state.astype(jnp.bfloat16).astype(jnp.float32), arrow_wide, precision=lax.Precision.HIGHEST)
    tip_state = jnp.dot(tip_side - arrow_total, tip_inverse.T, precision=lax.Precision.HIGHEST)
    tip_solution = jnp.dot(tip_state, tip_inverse, precision=lax.Precision.HIGHEST)
    backward_source = (forward_state - jnp.einsum("rf,tfs->trs", tip_solution, arrow_wide, precision=lax.Precision.HIGHEST)).astype(jnp.bfloat16)

    def backward_step(following, inputs):
        source_block, inverse_block, coupling_block, live_flag = inputs
        source = jnp.dot(source_block, inverse_block, preferred_element_type=jnp.float32)
        update = source - couple(following, coupling_block)
        state = jnp.where(live_flag, update, jnp.float32(0.0))
        following = jnp.where(live_flag, update, following)
        return following, state

    _, solution = lax.scan(backward_step, start, (backward_source, diag_inverse, backward_coupling, live_slot), reverse=True)
    return solution, tip_solution
```

```python
import functools

import jax
import jax.numpy as jnp
from jax import lax
from jax.experimental import pallas as pl
from jax.experimental.pallas import tpu as pltpu
from jax.sharding import Mesh
from jax.sharding import PartitionSpec as P

F32 = jnp.float32
BF16 = jnp.bfloat16
TM = ("za", "zb", "core")
SPACE = ("x", "y")
T = 4
R = 64
F = 8
W = 128
N = 16
G = R + F
HI = lax.Precision.HIGHEST


def split(x):
    high = x.astype(BF16)
    return high, (x - high.astype(F32)).astype(BF16)


def dot(a, b, dims):
    return lax.dot_general(a, b, ((dims[:1], dims[1:]), ((), ())), preferred_element_type=F32)


def times(x, m):
    xh, xl = split(x)
    mh, ml = split(m)
    return dot(jnp.concatenate([xh, xl, xh], 1), jnp.concatenate([mh, mh, ml], 0), (1, 0))


def times_t(x, c):
    xh, xl = split(x)
    return dot(jnp.concatenate([xh, xl], 1), jnp.concatenate([c, c], 1), (1, 1))


def eye(dtype):
    rows = lax.broadcasted_iota(jnp.int32, (W, W), 0)
    cols = lax.broadcasted_iota(jnp.int32, (W, W), 1)
    return jnp.where(rows == cols, 1.0, 0.0).astype(dtype)


def place():
    return tuple(lax.axis_index(name) for name in TM)


def live_count(sections):
    za, zb, core = place()
    return sections[(za * 4 + zb) * 2 + core]


def join(first, then):
    out = times(first, then[R : R + W])
    return jnp.concatenate([out[:R] + then[:R], out[R:]], 0)


def local_kernel(sections, side, inverse, forward, backward, states, maps, chunk):
    live = live_count(sections)
    state = None
    for t in range(T):
        driven = dot(side[t], inverse[t], (1, 1))
        if t == 0:
            state = jnp.concatenate([driven, -dot(eye(BF16), forward[0], (1, 1))], 0)
        else:
            moved = times_t(state, forward[t])
            state = jnp.where(
                t < live, jnp.concatenate([driven - moved[:R], -moved[R:]], 0), state
            )
        states[t] = state
    chunk[: R + W] = state
    mapping = eye(F32)
    for t in reversed(range(T)):
        mapping = jnp.where(t < live, -times_t(mapping, backward[t]), mapping)
        maps[t] = mapping
    chunk[R + W :] = mapping


def pair_kernel(own, other, out):
    _, _, core = place()
    first = jnp.where(core == 0, own[...], other[...])
    then = jnp.where(core == 0, other[...], own[...])
    both = join(first[: R + W], then[: R + W])
    back = times(then[R + W :], first[R + W :])
    for j in range(4):
        out[j, : R + W] = both
        out[j, R + W :] = back


def group_kernel(got, out, before, after):
    za, zb, _ = place()
    total = got[0, : R + W]
    before[...] = jnp.concatenate([jnp.zeros((R, W), F32), eye(F32)], 0)
    for j in range(1, 4):
        before[...] = jnp.where(zb == j, total, before[...])
        total = join(total, got[j, : R + W])
    back = got[3, R + W :]
    after[...] = eye(F32)
    for j in reversed(range(3)):
        after[...] = jnp.where(zb == j, back, after[...])
        back = times(back, got[j, R + W :])
    back = jnp.concatenate([back, jnp.zeros((R, W), F32)], 0)
    for j in range(4):
        out[j] = jnp.where(j > za, total, back)


def source_kernel(sections, got, before, other, states, inverse, arrow, out):
    za, _, core = place()
    live = live_count(sections)
    entry = jnp.where(za > 0, got[0, :R], 0.0)
    for j in range(1, 3):
        entry = jnp.where(j < za, times(entry, got[j, R:]) + got[j, :R], entry)
    entry = times(entry, before[R:]) + before[:R]
    entry = jnp.where(core == 1, times(entry, other[R : R + W]) + other[:R], entry)
    total = jnp.zeros((F, W), F32)
    pad = jnp.zeros((W - R, W), BF16)
    for t in range(T):
        state = states[t]
        state = jnp.where(t < live, state[:R] + times(entry, state[R:]), 0.0)
        high, low = split(state)
        total += dot(arrow[t], jnp.concatenate([high, pad], 0), (1, 1))
        rows = jnp.concatenate([high, low, arrow[t], jnp.zeros((F, W), BF16)], 0)
        terms = dot(rows, inverse[t], (1, 0))
        for n in range(N):
            cols = slice(n * W, (n + 1) * W)
            out[n, t * G : t * G + R] = terms[:R, cols] + terms[R : 2 * R, cols]
            out[n, t * G + R : (t + 1) * G] = terms[2 * R : 2 * R + F, cols]
    for n in range(N):
        out[n, T * G :] = total


def arrive_kernel(sections, got, backward, sums, chunk):
    live = live_count(sections)
    whole = got[0]
    for n in range(1, N):
        whole = whole + got[n]
    state = jnp.zeros((G, W), F32)
    for t in reversed(range(T)):
        source = whole[t * G : (t + 1) * G]
        state = jnp.where(t < live, source - times_t(state, backward[t]), state)
        sums[t] = state
    chunk[:G] = state
    chunk[G:] = whole[T * G :]


def back_pair_kernel(own, other, chunk, other_chunk, out):
    _, _, core = place()
    first = jnp.where(core == 0, own[...], other[...])
    then = jnp.where(core == 0, other[...], own[...])
    mapping = jnp.where(core == 0, chunk[R + W :], other_chunk[R + W :])
    state = times(then[:G], mapping) + first[:G]
    for j in range(4):
        out[j, :G] = state
        out[j, G:] = own[G:] + other[G:]


def back_group_kernel(got, maps, out, after):
    _, zb, _ = place()
    total = got[3, :G]
    after[...] = jnp.zeros((G, W), F32)
    for j in reversed(range(3)):
        after[...] = jnp.where(zb == j, total, after[...])
        total = times(total, maps[j, R + W :]) + got[j, :G]
    whole = ((got[0, G:] + got[1, G:]) + got[2, G:]) + got[3, G:]
    for j in range(4):
        out[j, :G] = total
        out[j, G:] = whole


def final_kernel(
    sections, got, totals, after, after_map, other, other_chunk, sums, maps, side, tip_inverse, out, tip_out
):
    za, _, core = place()
    live = live_count(sections)
    whole = ((got[0, G:] + got[1, G:]) + got[2, G:]) + got[3, G:]
    gap = side[...] - whole[:, :R]
    tip = lax.dot_general(
        tip_inverse[...], gap, (((1,), (0,)), ((), ())), precision=HI, preferred_element_type=F32
    )
    tip = lax.dot_general(
        tip_inverse[...], tip, (((0,), (0,)), ((), ())), precision=HI, preferred_element_type=F32
    )
    tip_out[...] = tip
    entry = jnp.where(za < 3, got[3, :G], 0.0)
    for j in (2, 1):
        entry = jnp.where(j > za, times(entry, totals[j, :W]) + got[j, :G], entry)
    entry = times(entry, after_map[...]) + after[...]
    entry = jnp.where(core == 0, times(entry, other_chunk[R + W :]) + other[:G], entry)
    tip_high, tip_low = split(tip)
    weights = jnp.concatenate(
        [tip_high.astype(F32), tip_low.astype(F32), tip_high.astype(F32)], 0
    ).astype(BF16)
    for t in range(T):
        state = sums[t] + times(entry, maps[t])
        high, low = split(state[R:])
        parts = jnp.concatenate([high.astype(F32), high.astype(F32), low.astype(F32)], 0).astype(BF16)
        out[t] = jnp.where(t < live, state[:R] - dot(weights, parts, (0, 0)), 0.0)


VMEM = pl.BlockSpec(memory_space=pltpu.VMEM)
SMEM = pl.BlockSpec(memory_space=pltpu.SMEM)


def call(kernel, shapes, *args):
    specs = [SMEM if a.dtype == jnp.int32 else VMEM for a in args]
    shapes = [jax.ShapeDtypeStruct(s, F32) for s in shapes]
    return pl.pallas_call(
        kernel,
        out_shape=shapes,
        in_specs=specs,
        out_specs=[VMEM] * len(shapes),
        name=kernel.__name__,
    )(*args)


def swap(a):
    return lax.ppermute(a, "core", [(0, 1), (1, 0)])


def exchange(a, axis):
    return lax.all_to_all(a, axis, 0, 0, tiled=True)


def on_device(
    sections, right_side, tip_side, diag_inverse, forward_coupling, backward_coupling, arrow_rows, tip_inverse
):
    states, maps, chunk = call(
        local_kernel,
        [(T, R + W, W), (T, W, W), (R + 2 * W, W)],
        sections,
        right_side,
        diag_inverse,
        forward_coupling,
        backward_coupling,
    )
    other_chunk = swap(chunk)
    (out,) = call(pair_kernel, [(4, R + 2 * W, W)], chunk, other_chunk)
    in_group = exchange(out, "zb")
    out, before, after_map = call(group_kernel, [(4, R + W, W), (R + W, W), (W, W)], in_group)
    totals = exchange(out, "za")
    (out,) = call(
        source_kernel,
        [(N, T * G + F, W)],
        sections,
        totals,
        before,
        other_chunk,
        states,
        diag_inverse,
        arrow_rows,
    )
    got = exchange(out, SPACE)
    sums, back_chunk = call(
        arrive_kernel, [(T, G, W), (G + F, W)], sections, got, backward_coupling
    )
    other_back = swap(back_chunk)
    (out,) = call(back_pair_kernel, [(4, G + F, W)], back_chunk, other_back, chunk, other_chunk)
    got = exchange(out, "zb")
    out, after = call(back_group_kernel, [(4, G + F, W), (G, W)], got, in_group)
    got = exchange(out, "za")
    solved, tip = call(
        final_kernel,
        [(T, R, W), (F, R)],
        sections,
        got,
        totals,
        after,
        after_map,
        other_back,
        other_chunk,
        sums,
        maps,
        tip_side.T,
        tip_inverse,
    )
    return solved, tip.T


def solution(mesh):
    torus = Mesh(mesh.devices.reshape(4, 4, 2, 4, 4), TM + SPACE)
    return jax.shard_map(
        on_device,
        mesh=torus,
        in_specs=(
            P(),
            P(TM, None, None),
            P(),
            P(TM, SPACE, None),
            P(TM, SPACE, None),
            P(TM, SPACE, None),
            P(TM, None, SPACE),
            P(),
        ),
        out_specs=(P(TM, None, SPACE), P()),
        check_vma=False,
    )
```

```python
import functools

import jax
import jax.numpy as jnp
from jax import lax
from jax.experimental import pallas as pl
from jax.experimental.pallas import tpu as pltpu
from jax.sharding import Mesh
from jax.sharding import PartitionSpec as P

F32 = jnp.float32
BF16 = jnp.bfloat16
TM = ("za", "zb", "core")
SPACE = ("x", "y")
T = 4
R = 64
F = 8
W = 128
N = 16
G = R + F
HI = lax.Precision.HIGHEST


def split(x):
    high = x.astype(BF16)
    return high, (x - high.astype(F32)).astype(BF16)


def dot(a, b, dims):
    return lax.dot_general(a, b, ((dims[:1], dims[1:]), ((), ())), preferred_element_type=F32)


def times(x, m):
    xh, xl = split(x)
    mh, ml = split(m)
    return dot(jnp.concatenate([xh, xl, xh], 1), jnp.concatenate([mh, mh, ml], 0), (1, 0))


def times_t(x, c):
    xh, xl = split(x)
    return dot(jnp.concatenate([xh, xl], 1), jnp.concatenate([c, c], 1), (1, 1))


def eye(dtype):
    rows = lax.broadcasted_iota(jnp.int32, (W, W), 0)
    cols = lax.broadcasted_iota(jnp.int32, (W, W), 1)
    return jnp.where(rows == cols, 1.0, 0.0).astype(dtype)


def place():
    return tuple(lax.axis_index(name) for name in TM)


def live_count(sections):
    za, zb, core = place()
    return sections[(za * 4 + zb) * 2 + core]


def join(first, then):
    out = times(first, then[R : R + W])
    return jnp.concatenate([out[:R] + then[:R], out[R:]], 0)


def local_kernel(sections, side, inverse, forward, backward, states, maps, chunk):
    live = live_count(sections)
    state = None
    for t in range(T):
        driven = dot(side[t], inverse[t], (1, 1))
        if t == 0:
            state = jnp.concatenate([driven, -dot(eye(BF16), forward[0], (1, 1))], 0)
        else:
            moved = times_t(state, forward[t])
            state = jnp.where(
                t < live, jnp.concatenate([driven - moved[:R], -moved[R:]], 0), state
            )
        states[t] = state
    chunk[: R + W] = state
    mapping = eye(F32)
    for t in reversed(range(T)):
        mapping = jnp.where(t < live, -times_t(mapping, backward[t]), mapping)
        maps[t] = mapping
    chunk[R + W :] = mapping


def pair_kernel(own, other, out):
    _, _, core = place()
    first = jnp.where(core == 0, own[...], other[...])
    then = jnp.where(core == 0, other[...], own[...])
    both = join(first[: R + W], then[: R + W])
    back = times(then[R + W :], first[R + W :])
    for j in range(4):
        out[j, : R + W] = both
        out[j, R + W :] = back


def group_kernel(got, out, before, after):
    za, zb, _ = place()
    total = got[0, : R + W]
    before[...] = jnp.concatenate([jnp.zeros((R, W), F32), eye(F32)], 0)
    for j in range(1, 4):
        before[...] = jnp.where(zb == j, total, before[...])
        total = join(total, got[j, : R + W])
    back = got[3, R + W :]
    after[...] = eye(F32)
    for j in reversed(range(3)):
        after[...] = jnp.where(zb == j, back, after[...])
        back = times(back, got[j, R + W :])
    back = jnp.concatenate([back, jnp.zeros((R, W), F32)], 0)
    for j in range(4):
        out[j] = jnp.where(j > za, total, back)


def source_kernel(sections, got, before, other, states, inverse, arrow, out):
    za, _, core = place()
    live = live_count(sections)
    entry = jnp.where(za > 0, got[0, :R], 0.0)
    for j in range(1, 3):
        entry = jnp.where(j < za, times(entry, got[j, R:]) + got[j, :R], entry)
    entry = times(entry, before[R:]) + before[:R]
    entry = jnp.where(core == 1, times(entry, other[R : R + W]) + other[:R], entry)
    total = jnp.zeros((F, W), F32)
    pad = jnp.zeros((W - R, W), BF16)
    for t in range(T):
        state = states[t]
        state = jnp.where(t < live, state[:R] + times(entry, state[R:]), 0.0)
        high, low = split(state)
        total += dot(arrow[t], jnp.concatenate([high, pad], 0), (1, 1))
        rows = jnp.concatenate([high, low, arrow[t], jnp.zeros((F, W), BF16)], 0)
        terms = dot(rows, inverse[t], (1, 0))
        for n in range(N):
            cols = slice(n * W, (n + 1) * W)
            out[n, t * G : t * G + R] = terms[:R, cols] + terms[R : 2 * R, cols]
            out[n, t * G + R : (t + 1) * G] = terms[2 * R : 2 * R + F, cols]
    for n in range(N):
        out[n, T * G :] = total


def arrive_kernel(sections, got, backward, sums, chunk):
    live = live_count(sections)
    whole = got[0]
    for n in range(1, N):
        whole = whole + got[n]
    state = jnp.zeros((G, W), F32)
    for t in reversed(range(T)):
        source = whole[t * G : (t + 1) * G]
        state = jnp.where(t < live, source - times_t(state, backward[t]), state)
        sums[t] = state
    chunk[:G] = state
    chunk[G:] = whole[T * G :]


def back_pair_kernel(own, other, chunk, other_chunk, out):
    _, _, core = place()
    first = jnp.where(core == 0, own[...], other[...])
    then = jnp.where(core == 0, other[...], own[...])
    mapping = jnp.where(core == 0, chunk[R + W :], other_chunk[R + W :])
    state = times(then[:G], mapping) + first[:G]
    for j in range(4):
        out[j, :G] = state
        out[j, G:] = own[G:] + other[G:]


def back_group_kernel(got, maps, out, after):
    _, zb, _ = place()
    total = got[3, :G]
    after[...] = jnp.zeros((G, W), F32)
    for j in reversed(range(3)):
        after[...] = jnp.where(zb == j, total, after[...])
        total = times(total, maps[j, R + W :]) + got[j, :G]
    whole = ((got[0, G:] + got[1, G:]) + got[2, G:]) + got[3, G:]
    for j in range(4):
        out[j, :G] = total
        out[j, G:] = whole


def final_kernel(
    sections, got, totals, after, after_map, other, other_chunk, sums, maps, side, tip_inverse, out, tip_out
):
    za, _, core = place()
    live = live_count(sections)
    whole = ((got[0, G:] + got[1, G:]) + got[2, G:]) + got[3, G:]
    gap = side[...] - whole[:, :R]
    tip = lax.dot_general(
        tip_inverse[...], gap, (((1,), (0,)), ((), ())), precision=HI, preferred_element_type=F32
    )
    tip = lax.dot_general(
        tip_inverse[...], tip, (((0,), (0,)), ((), ())), precision=HI, preferred_element_type=F32
    )
    tip_out[...] = tip
    entry = jnp.where(za < 3, got[3, :G], 0.0)
    for j in (2, 1):
        entry = jnp.where(j > za, times(entry, totals[j, :W]) + got[j, :G], entry)
    entry = times(entry, after_map[...]) + after[...]
    entry = jnp.where(core == 0, times(entry, other_chunk[R + W :]) + other[:G], entry)
    tip_high, tip_low = split(tip)
    weights = jnp.concatenate(
        [tip_high.astype(F32), tip_low.astype(F32), tip_high.astype(F32)], 0
    ).astype(BF16)
    for t in range(T):
        state = sums[t] + times(entry, maps[t])
        high, low = split(state[R:])
        parts = jnp.concatenate([high.astype(F32), high.astype(F32), low.astype(F32)], 0).astype(BF16)
        out[t] = jnp.where(t < live, state[:R] - dot(weights, parts, (0, 0)), 0.0)


VMEM = pl.BlockSpec(memory_space=pltpu.VMEM)
SMEM = pl.BlockSpec(memory_space=pltpu.SMEM)


def call(kernel, shapes, *args):
    specs = [SMEM if a.dtype == jnp.int32 else VMEM for a in args]
    shapes = [jax.ShapeDtypeStruct(s, F32) for s in shapes]
    return pl.pallas_call(
        kernel,
        out_shape=shapes,
        in_specs=specs,
        out_specs=[VMEM] * len(shapes),
        compiler_params=pltpu.CompilerParams(vmem_limit_bytes=16 << 20),
        name=kernel.__name__,
    )(*args)


def swap(a):
    return lax.ppermute(a, "core", [(0, 1), (1, 0)])


def exchange(a, axis):
    return lax.all_to_all(a, axis, 0, 0, tiled=True)


def on_device(
    sections, right_side, tip_side, diag_inverse, forward_coupling, backward_coupling, arrow_rows, tip_inverse
):
    states, maps, chunk = call(
        local_kernel,
        [(T, R + W, W), (T, W, W), (R + 2 * W, W)],
        sections,
        right_side,
        diag_inverse,
        forward_coupling,
        backward_coupling,
    )
    other_chunk = swap(chunk)
    (out,) = call(pair_kernel, [(4, R + 2 * W, W)], chunk, other_chunk)
    in_group = exchange(out, "zb")
    out, before, after_map = call(group_kernel, [(4, R + W, W), (R + W, W), (W, W)], in_group)
    totals = exchange(out, "za")
    (out,) = call(
        source_kernel,
        [(N, T * G + F, W)],
        sections,
        totals,
        before,
        other_chunk,
        states,
        diag_inverse,
        arrow_rows,
    )
    got = exchange(out, SPACE)
    sums, back_chunk = call(
        arrive_kernel, [(T, G, W), (G + F, W)], sections, got, backward_coupling
    )
    other_back = swap(back_chunk)
    (out,) = call(back_pair_kernel, [(4, G + F, W)], back_chunk, other_back, chunk, other_chunk)
    got = exchange(out, "zb")
    out, after = call(back_group_kernel, [(4, G + F, W), (G, W)], got, in_group)
    got = exchange(out, "za")
    solved, tip = call(
        final_kernel,
        [(T, R, W), (F, R)],
        sections,
        got,
        totals,
        after,
        after_map,
        other_back,
        other_chunk,
        sums,
        maps,
        tip_side.T,
        tip_inverse,
    )
    return solved, tip.T


def solution(mesh):
    torus = Mesh(mesh.devices.reshape(4, 4, 2, 4, 4), TM + SPACE)
    return jax.shard_map(
        on_device,
        mesh=torus,
        in_specs=(
            P(),
            P(TM, None, None),
            P(),
            P(TM, SPACE, None),
            P(TM, SPACE, None),
            P(TM, SPACE, None),
            P(TM, None, SPACE),
            P(),
        ),
        out_specs=(P(TM, None, SPACE), P()),
        check_vma=False,
    )
```

```python
import jax
import jax.numpy as jnp
from jax import lax
from jax.experimental import pallas as pl
from jax.experimental.pallas import tpu as pltpu
from jax.sharding import Mesh
from jax.sharding import PartitionSpec as P

F32 = jnp.float32
BF16 = jnp.bfloat16
TM = ("zg", "zp", "core")
SPACE = ("x", "y")
NEAR = ("zp", "core")
FAR = ("zg", "core")
T = 4
R = 64
F = 8
W = 128
N = 16
G = R + F
L = 4
Q = 8
HI = lax.Precision.HIGHEST


def split(x):
    high = x.astype(BF16)
    return high, (x - high.astype(F32)).astype(BF16)


def dot(a, b, dims):
    return lax.dot_general(a, b, ((dims[:1], dims[1:]), ((), ())), preferred_element_type=F32)


def times(x, m):
    xh, xl = split(x)
    mh, ml = split(m)
    return dot(jnp.concatenate([xh, xl, xh], 1), jnp.concatenate([mh, mh, ml], 0), (1, 0))


def times_t(x, c):
    xh, xl = split(x)
    return dot(jnp.concatenate([xh, xl], 1), jnp.concatenate([c, c], 1), (1, 1))


def eye(dtype):
    rows = lax.broadcasted_iota(jnp.int32, (W, W), 0)
    cols = lax.broadcasted_iota(jnp.int32, (W, W), 1)
    return jnp.where(rows == cols, 1.0, 0.0).astype(dtype)


def near_index():
    return lax.axis_index("zp") * 2 + lax.axis_index("core")


def live_count(sections):
    return sections[lax.axis_index("zg") * L + near_index()]


def join(first, then):
    out = times(first, then[R : R + W])
    return jnp.concatenate([out[:R] + then[:R], out[R:]], 0)


def half_of(x):
    rows = x.shape[0] // 2
    return jnp.where(lax.axis_index("core") == 0, x[:rows], x[rows:])


def local_kernel(
    sections_in, side_in, inverse_in, forward_in, states, chunk, sections, side, inverse, forward, sems
):
    copies = [
        pltpu.make_async_copy(sections_in, sections, sems.at[0]),
        pltpu.make_async_copy(forward_in, forward, sems.at[1]),
    ]
    for t in range(T):
        copies.append(pltpu.make_async_copy(side_in.at[t], side.at[t], sems.at[2 + 2 * t]))
        copies.append(pltpu.make_async_copy(inverse_in.at[t], inverse.at[t], sems.at[3 + 2 * t]))
    for copy in copies:
        copy.start()
    copies[0].wait()
    copies[1].wait()
    live = live_count(sections)
    state = None
    for t in range(T):
        copies[2 + 2 * t].wait()
        copies[3 + 2 * t].wait()
        driven = dot(side[t], inverse[t], (1, 1))
        if t == 0:
            state = jnp.concatenate([driven, -dot(eye(BF16), forward[0], (1, 1))], 0)
        else:
            moved = times_t(state, forward[t])
            state = jnp.where(
                t < live, jnp.concatenate([driven - moved[:R], -moved[R:]], 0), state
            )
        states[t] = state
    chunk[...] = state


def group_kernel(got, out, before):
    me = near_index()
    total = got[0]
    before[...] = jnp.concatenate([jnp.zeros((R, W), F32), eye(F32)], 0)
    for j in range(1, L):
        before[...] = jnp.where(me == j, total, before[...])
        total = join(total, got[j])
    out[...] = half_of(total)


def source_kernel(sections, got, before, states, inverse, arrow, out):
    group = lax.axis_index("zg")
    live = live_count(sections)
    entry = jnp.where(group > 0, got[0, :R], 0.0)
    for j in range(1, Q - 1):
        mapping = jnp.concatenate([got[2 * j, R:], got[2 * j + 1]], 0)
        entry = jnp.where(j < group, times(entry, mapping) + got[2 * j, :R], entry)
    entry = times(entry, before[R:]) + before[:R]
    total = jnp.zeros((F, W), F32)
    pad = jnp.zeros((W - R, W), BF16)
    for t in range(T):
        state = states[t]
        state = jnp.where(t < live, state[:R] + times(entry, state[R:]), 0.0)
        high, low = split(state)
        total += dot(arrow[t], jnp.concatenate([high, pad], 0), (1, 1))
        rows = jnp.concatenate([high, low, arrow[t], jnp.zeros((F, W), BF16)], 0)
        terms = dot(rows, inverse[t], (1, 0))
        for n in range(N):
            cols = slice(n * W, (n + 1) * W)
            out[n, t * G : t * G + R] = terms[:R, cols] + terms[R : 2 * R, cols]
            out[n, t * G + R : (t + 1) * G] = terms[2 * R : 2 * R + F, cols]
    for n in range(N):
        out[n, T * G :] = total


def maps_kernel(sections, backward, maps, chunk):
    live = live_count(sections)
    mapping = eye(F32)
    for t in reversed(range(T)):
        mapping = jnp.where(t < live, -times_t(mapping, backward[t]), mapping)
        maps[t] = mapping
    chunk[...] = mapping


def group_maps_kernel(got, out, after):
    me = near_index()
    total = got[L - 1]
    after[...] = eye(F32)
    for j in reversed(range(L - 1)):
        after[...] = jnp.where(me == j, total, after[...])
        total = times(total, got[j])
    out[...] = half_of(total)


def arrive_kernel(sections, got, backward, sums, chunk):
    live = live_count(sections)
    whole = got[0]
    for n in range(1, N):
        whole = whole + got[n]
    state = jnp.zeros((G, W), F32)
    for t in reversed(range(T)):
        source = whole[t * G : (t + 1) * G]
        state = jnp.where(t < live, source - times_t(state, backward[t]), state)
        sums[t] = state
    chunk[:G] = state
    chunk[G:] = whole[T * G :]


def back_group_kernel(got, maps, out, after):
    me = near_index()
    total = got[L - 1, :G]
    after[...] = jnp.zeros((G, W), F32)
    for j in reversed(range(L - 1)):
        after[...] = jnp.where(me == j, total, after[...])
        total = times(total, maps[j]) + got[j, :G]
    whole = ((got[0, G:] + got[1, G:]) + got[2, G:]) + got[3, G:]
    out[...] = half_of(jnp.concatenate([total, whole], 0))


def final_kernel(
    sections, got, totals, after, after_map, sums, maps, side, tip_inverse, out, tip_out
):
    group = lax.axis_index("zg")
    live = live_count(sections)
    edge = (G + F) // 2
    whole = got[1, edge - F :]
    for j in range(1, Q):
        whole = whole + got[2 * j + 1, edge - F :]
    gap = side[...] - whole[:, :R]
    tip = lax.dot_general(
        tip_inverse[...], gap, (((1,), (0,)), ((), ())), precision=HI, preferred_element_type=F32
    )
    tip = lax.dot_general(
        tip_inverse[...], tip, (((0,), (0,)), ((), ())), precision=HI, preferred_element_type=F32
    )
    tip_out[...] = tip

    def offset(j):
        return jnp.concatenate([got[2 * j], got[2 * j + 1, : edge - F]], 0)

    entry = jnp.where(group < Q - 1, offset(Q - 1), 0.0)
    for j in reversed(range(1, Q - 1)):
        mapping = jnp.concatenate([totals[2 * j], totals[2 * j + 1]], 0)
        entry = jnp.where(j > group, times(entry, mapping) + offset(j), entry)
    entry = times(entry, after_map[...]) + after[...]
    tip_high, tip_low = split(tip)
    weights = jnp.concatenate(
        [tip_high.astype(F32), tip_low.astype(F32), tip_high.astype(F32)], 0
    ).astype(BF16)
    for t in range(T):
        state = sums[t] + times(entry, maps[t])
        high, low = split(state[R:])
        parts = jnp.concatenate([high.astype(F32), high.astype(F32), low.astype(F32)], 0).astype(BF16)
        out[t] = jnp.where(t < live, state[:R] - dot(weights, parts, (0, 0)), 0.0)


VMEM = pl.BlockSpec(memory_space=pltpu.VMEM)
SMEM = pl.BlockSpec(memory_space=pltpu.SMEM)
HBM = pl.BlockSpec(memory_space=pltpu.HBM)


def call(kernel, shapes, *args, own_copies=False, scratch=()):
    specs = [HBM if own_copies else SMEM if a.dtype == jnp.int32 else VMEM for a in args]
    shapes = [jax.ShapeDtypeStruct(s, F32) for s in shapes]
    return pl.pallas_call(
        kernel,
        out_shape=shapes,
        in_specs=specs,
        out_specs=[VMEM] * len(shapes),
        scratch_shapes=scratch,
        compiler_params=pltpu.CompilerParams(vmem_limit_bytes=16 << 20),
    )(*args)


def on_device(
    sections, right_side, tip_side, diag_inverse, forward_coupling, backward_coupling, arrow_rows, tip_inverse
):
    states, chunk = call(
        local_kernel,
        [(T, R + W, W), (R + W, W)],
        sections,
        right_side,
        diag_inverse,
        forward_coupling,
        own_copies=True,
        scratch=(
            pltpu.SMEM(sections.shape, jnp.int32),
            pltpu.VMEM(right_side.shape, BF16),
            pltpu.VMEM(diag_inverse.shape, BF16),
            pltpu.VMEM(forward_coupling.shape, BF16),
            pltpu.SemaphoreType.DMA((2 + 2 * T,)),
        ),
    )
    got = lax.all_gather(chunk, NEAR)
    out, before = call(group_kernel, [((R + W) // 2, W), (R + W, W)], got)
    got = lax.all_gather(out, FAR)
    (out,) = call(
        source_kernel,
        [(N, T * G + F, W)],
        sections,
        got,
        before,
        states,
        diag_inverse,
        arrow_rows,
    )
    got = lax.all_to_all(out, SPACE, 0, 0, tiled=True)
    maps, chunk = call(maps_kernel, [(T, W, W), (W, W)], sections, backward_coupling)
    near_maps = lax.all_gather(chunk, NEAR)
    out, after_map = call(group_maps_kernel, [(W // 2, W), (W, W)], near_maps)
    far_maps = lax.all_gather(out, FAR)
    sums, chunk = call(arrive_kernel, [(T, G, W), (G + F, W)], sections, got, backward_coupling)
    got = lax.all_gather(chunk, NEAR)
    out, after = call(back_group_kernel, [((G + F) // 2, W), (G, W)], got, near_maps)
    got = lax.all_gather(out, FAR)
    solved, tip = call(
        final_kernel,
        [(T, R, W), (F, R)],
        sections,
        got,
        far_maps,
        after,
        after_map,
        sums,
        maps,
        tip_side.T,
        tip_inverse,
    )
    return solved, tip.T


def solution(mesh):
    torus = Mesh(mesh.devices.reshape(Q, 2, 2, 4, 4), TM + SPACE)
    return jax.shard_map(
        on_device,
        mesh=torus,
        in_specs=(
            P(),
            P(TM, None, None),
            P(),
            P(TM, SPACE, None),
            P(TM, SPACE, None),
            P(TM, SPACE, None),
            P(TM, None, SPACE),
            P(),
        ),
        out_specs=(P(TM, None, SPACE), P()),
        check_vma=False,
    )
```

```python
import functools

import jax
import jax.numpy as jnp
from jax import lax
from jax.experimental import pallas as pl
from jax.experimental.pallas import tpu as pltpu
from jax.sharding import Mesh
from jax.sharding import PartitionSpec as P

F32 = jnp.float32
BF16 = jnp.bfloat16
TM = ("zg", "zp", "core")
SPACE = ("x", "y")
NEAR = ("zp", "core")
FAR = ("zg", "core")
T = 4
R = 64
F = 8
W = 128
N = 16
G = R + F
L = 4
Q = 8
EDGE = (G + F) // 2
GRANT = 66_000_000
HI = lax.Precision.HIGHEST


def split(x):
    high = x.astype(BF16)
    return high, (x - high.astype(F32)).astype(BF16)


def dot(a, b, dims):
    return lax.dot_general(a, b, ((dims[:1], dims[1:]), ((), ())), preferred_element_type=F32)


def times(x, m):
    xh, xl = split(x)
    mh, ml = split(m)
    return dot(jnp.concatenate([xh, xl, xh], 1), jnp.concatenate([mh, mh, ml], 0), (1, 0))


def times_t(x, c):
    xh, xl = split(x)
    return dot(jnp.concatenate([xh, xl], 1), jnp.concatenate([c, c], 1), (1, 1))


def eye(dtype):
    rows = lax.broadcasted_iota(jnp.int32, (W, W), 0)
    cols = lax.broadcasted_iota(jnp.int32, (W, W), 1)
    return jnp.where(rows == cols, 1.0, 0.0).astype(dtype)


def near_index():
    return lax.axis_index("zp") * 2 + lax.axis_index("core")


def live_count(sections):
    return sections[lax.axis_index("zg") * L + near_index()]


def join(first, then):
    out = times(first, then[R : R + W])
    return jnp.concatenate([out[:R] + then[:R], out[R:]], 0)


def half_of(x):
    rows = x.shape[0] // 2
    return jnp.where(lax.axis_index("core") == 0, x[:rows], x[rows:])


def local_kernel(
    sections_in,
    side_in,
    inverse_in,
    forward_in,
    backward_in,
    states,
    maps,
    chunk,
    sections,
    side,
    inverse,
    forward,
    backward,
    sems,
):
    copies = [
        pltpu.make_async_copy(sections_in, sections, sems.at[0]),
        pltpu.make_async_copy(backward_in, backward, sems.at[1]),
        pltpu.make_async_copy(forward_in, forward, sems.at[2]),
    ]
    for t in range(T):
        copies.append(pltpu.make_async_copy(side_in.at[t], side.at[t], sems.at[3 + 2 * t]))
        copies.append(pltpu.make_async_copy(inverse_in.at[t], inverse.at[t], sems.at[4 + 2 * t]))
    for copy in copies:
        copy.start()
    for copy in copies[:3]:
        copy.wait()
    live = live_count(sections)
    mapping = eye(F32)
    for t in reversed(range(T)):
        mapping = jnp.where(t < live, -times_t(mapping, backward[t]), mapping)
        maps[t] = mapping
    chunk[R + W :] = mapping
    state = None
    for t in range(T):
        copies[3 + 2 * t].wait()
        copies[4 + 2 * t].wait()
        driven = dot(side[t], inverse[t], (1, 1))
        if t == 0:
            state = jnp.concatenate([driven, -dot(eye(BF16), forward[0], (1, 1))], 0)
        else:
            moved = times_t(state, forward[t])
            state = jnp.where(
                t < live, jnp.concatenate([driven - moved[:R], -moved[R:]], 0), state
            )
        states[t] = state
    chunk[: R + W] = state


def group_kernel(got, out, back, before, after):
    me = near_index()
    total = got[0, : R + W]
    before[...] = jnp.concatenate([jnp.zeros((R, W), F32), eye(F32)], 0)
    mapping = got[L - 1, R + W :]
    after[...] = eye(F32)
    for j in range(1, L):
        before[...] = jnp.where(me == j, total, before[...])
        total = join(total, got[j, : R + W])
        after[...] = jnp.where(me == L - 1 - j, mapping, after[...])
        mapping = times(mapping, got[L - 1 - j, R + W :])
    out[...] = half_of(total)
    back[...] = half_of(mapping)


def source_kernel(sections, got, before, states, inverse, arrow, out):
    group = lax.axis_index("zg")
    live = live_count(sections)
    entry = jnp.where(group > 0, got[0, :R], 0.0)
    for j in range(1, Q - 1):
        mapping = jnp.concatenate([got[2 * j, R:], got[2 * j + 1]], 0)
        entry = jnp.where(j < group, times(entry, mapping) + got[2 * j, :R], entry)
    entry = times(entry, before[R:]) + before[:R]
    total = jnp.zeros((F, W), F32)
    pad = jnp.zeros((W - R, W), BF16)
    for t in range(T):
        state = states[t]
        state = jnp.where(t < live, state[:R] + times(entry, state[R:]), 0.0)
        high, low = split(state)
        total += dot(arrow[t], jnp.concatenate([high, pad], 0), (1, 1))
        rows = jnp.concatenate([high, low, arrow[t], jnp.zeros((F, W), BF16)], 0)
        terms = dot(rows, inverse[t], (1, 0))
        for n in range(N):
            cols = slice(n * W, (n + 1) * W)
            out[n, t * G : t * G + R] = terms[:R, cols] + terms[R : 2 * R, cols]
            out[n, t * G + R : (t + 1) * G] = terms[2 * R : 2 * R + F, cols]
    for n in range(N):
        out[n, T * G :] = total


def arrive_kernel(sections, got, backward, sums, chunk):
    live = live_count(sections)
    whole = got[0]
    for n in range(1, N):
        whole = whole + got[n]
    state = jnp.zeros((G, W), F32)
    for t in reversed(range(T)):
        source = whole[t * G : (t + 1) * G]
        state = jnp.where(t < live, source - times_t(state, backward[t]), state)
        sums[t] = state
    chunk[:G] = state
    chunk[G:] = whole[T * G :]


def back_group_kernel(got, maps, mapping, out, after):
    me = near_index()
    total = got[L - 1, :G]
    after[...] = jnp.zeros((G, W), F32)
    for j in reversed(range(L - 1)):
        after[...] = jnp.where(me == j, total, after[...])
        total = times(total, maps[j, R + W :]) + got[j, :G]
    whole = ((got[0, G:] + got[1, G:]) + got[2, G:]) + got[3, G:]
    out[:EDGE] = half_of(jnp.concatenate([total, whole], 0))
    out[EDGE:] = mapping[...]


def final_kernel(
    sections, got, after, after_map, sums, maps, side, tip_inverse, out, tip_out
):
    group = lax.axis_index("zg")
    live = live_count(sections)
    whole = got[1, EDGE - F : EDGE]
    for j in range(1, Q):
        whole = whole + got[2 * j + 1, EDGE - F : EDGE]
    gap = side[...] - whole[:, :R]
    tip = lax.dot_general(
        tip_inverse[...], gap, (((1,), (0,)), ((), ())), precision=HI, preferred_element_type=F32
    )
    tip = lax.dot_general(
        tip_inverse[...], tip, (((0,), (0,)), ((), ())), precision=HI, preferred_element_type=F32
    )
    tip_out[...] = tip

    def offset(j):
        return jnp.concatenate([got[2 * j, :EDGE], got[2 * j + 1, : EDGE - F]], 0)

    entry = jnp.where(group < Q - 1, offset(Q - 1), 0.0)
    for j in reversed(range(1, Q - 1)):
        mapping = jnp.concatenate([got[2 * j, EDGE:], got[2 * j + 1, EDGE:]], 0)
        entry = jnp.where(j > group, times(entry, mapping) + offset(j), entry)
    entry = times(entry, after_map[...]) + after[...]
    tip_high, tip_low = split(tip)
    weights = jnp.concatenate(
        [tip_high.astype(F32), tip_low.astype(F32), tip_high.astype(F32)], 0
    ).astype(BF16)
    for t in range(T):
        state = sums[t] + times(entry, maps[t])
        high, low = split(state[R:])
        parts = jnp.concatenate([high.astype(F32), high.astype(F32), low.astype(F32)], 0).astype(BF16)
        out[t] = jnp.where(t < live, state[:R] - dot(weights, parts, (0, 0)), 0.0)


VMEM = pl.BlockSpec(memory_space=pltpu.VMEM)
SMEM = pl.BlockSpec(memory_space=pltpu.SMEM)
HBM = pl.BlockSpec(memory_space=pltpu.HBM)


def call(kernel, shapes, *args, own_copies=False, scratch=(), grant=16 << 20):
    specs = [HBM if own_copies else SMEM if a.dtype == jnp.int32 else VMEM for a in args]
    shapes = [jax.ShapeDtypeStruct(s, F32) for s in shapes]
    return pl.pallas_call(
        kernel,
        out_shape=shapes,
        in_specs=specs,
        out_specs=[VMEM] * len(shapes),
        scratch_shapes=scratch,
        compiler_params=pltpu.CompilerParams(vmem_limit_bytes=grant),
        name=kernel.__name__,
    )(*args)


def on_device(
    sections, right_side, tip_side, diag_inverse, forward_coupling, backward_coupling, arrow_rows, tip_inverse
):
    states, maps, chunk = call(
        local_kernel,
        [(T, R + W, W), (T, W, W), (R + 2 * W, W)],
        sections,
        right_side,
        diag_inverse,
        forward_coupling,
        backward_coupling,
        own_copies=True,
        scratch=(
            pltpu.SMEM(sections.shape, jnp.int32),
            pltpu.VMEM(right_side.shape, BF16),
            pltpu.VMEM(diag_inverse.shape, BF16),
            pltpu.VMEM(forward_coupling.shape, BF16),
            pltpu.VMEM(backward_coupling.shape, BF16),
            pltpu.SemaphoreType.DMA((3 + 2 * T,)),
        ),
        grant=GRANT,
    )
    near = lax.all_gather(chunk, NEAR)
    out, back, before, after_map = call(
        group_kernel, [((R + W) // 2, W), (W // 2, W), (R + W, W), (W, W)], near
    )
    got = lax.all_gather(out, FAR)
    (out,) = call(
        source_kernel,
        [(N, T * G + F, W)],
        sections,
        got,
        before,
        states,
        diag_inverse,
        arrow_rows,
    )
    got = lax.all_to_all(out, SPACE, 0, 0, tiled=True)
    sums, chunk = call(arrive_kernel, [(T, G, W), (G + F, W)], sections, got, backward_coupling)
    got = lax.all_gather(chunk, NEAR)
    out, after = call(back_group_kernel, [(EDGE + W // 2, W), (G, W)], got, near, back)
    got = lax.all_gather(out, FAR)
    solved, tip = call(
        final_kernel,
        [(T, R, W), (F, R)],
        sections,
        got,
        after,
        after_map,
        sums,
        maps,
        tip_side.T,
        tip_inverse,
    )
    return solved, tip.T


def solution(mesh):
    torus = Mesh(mesh.devices.reshape(Q, 2, 2, 4, 4), TM + SPACE)
    return jax.shard_map(
        on_device,
        mesh=torus,
        in_specs=(
            P(),
            P(TM, None, None),
            P(),
            P(TM, SPACE, None),
            P(TM, SPACE, None),
            P(TM, SPACE, None),
            P(TM, None, SPACE),
            P(),
        ),
        out_specs=(P(TM, None, SPACE), P()),
        check_vma=False,
    )
```

```python
import functools

import jax
import jax.numpy as jnp
from jax import lax
from jax.experimental import pallas as pl
from jax.experimental.pallas import tpu as pltpu
from jax.sharding import Mesh
from jax.sharding import PartitionSpec as P

F32 = jnp.float32
BF16 = jnp.bfloat16
TM = ("zg", "zp", "core")
SPACE = ("x", "y")
NEAR = ("zp", "core")
FAR = ("zg", "core")
T = 4
R = 64
F = 8
W = 128
N = 16
G = R + F
L = 4
Q = 8
EDGE = (G + F) // 2
HI = lax.Precision.HIGHEST


def split(x):
    high = x.astype(BF16)
    return high, (x - high.astype(F32)).astype(BF16)


def dot(a, b, dims):
    return lax.dot_general(a, b, ((dims[:1], dims[1:]), ((), ())), preferred_element_type=F32)


def times(x, m):
    xh, xl = split(x)
    mh, ml = split(m)
    return dot(jnp.concatenate([xh, xl, xh], 1), jnp.concatenate([mh, mh, ml], 0), (1, 0))


def times_t(x, c):
    xh, xl = split(x)
    return dot(jnp.concatenate([xh, xl], 1), jnp.concatenate([c, c], 1), (1, 1))


def eye(dtype):
    rows = lax.broadcasted_iota(jnp.int32, (W, W), 0)
    cols = lax.broadcasted_iota(jnp.int32, (W, W), 1)
    return jnp.where(rows == cols, 1.0, 0.0).astype(dtype)


def near_index():
    return lax.axis_index("zp") * 2 + lax.axis_index("core")


def live_count(sections):
    return sections[lax.axis_index("zg") * L + near_index()]


def join(first, then, rows=R):
    out = times(first, then[rows:])
    return jnp.concatenate([out[:rows] + then[:rows], out[rows:]], 0)


def offset_of(parts, rows):
    ahead = times(parts[0][:rows], parts[1][rows:]) + parts[1][:rows]
    middle = join(parts[2], parts[3], rows)
    behind = join(join(parts[4], parts[5], rows), parts[6], rows)
    ahead = times(ahead, middle[rows:]) + middle[:rows]
    return times(ahead, behind[rows:]) + behind[:rows]


def kept(flag, part, rows):
    neutral = jnp.concatenate([jnp.zeros((rows, W), F32), eye(F32)], 0)
    return jnp.where(flag, part, neutral)


def half_of(x):
    rows = x.shape[0] // 2
    return jnp.where(lax.axis_index("core") == 0, x[:rows], x[rows:])


def local_kernel(
    sections_in,
    side_in,
    inverse_in,
    forward_in,
    backward_in,
    states,
    maps,
    chunk,
    inverse,
    backward,
    sections,
    side,
    forward,
    sems,
):
    copies = [
        pltpu.make_async_copy(sections_in, sections, sems.at[0]),
        pltpu.make_async_copy(backward_in, backward, sems.at[1]),
        pltpu.make_async_copy(forward_in, forward, sems.at[2]),
    ]
    for t in range(T):
        copies.append(pltpu.make_async_copy(side_in.at[t], side.at[t], sems.at[3 + 2 * t]))
        copies.append(pltpu.make_async_copy(inverse_in.at[t], inverse.at[t], sems.at[4 + 2 * t]))
    for copy in copies:
        copy.start()
    for copy in copies[:3]:
        copy.wait()
    live = live_count(sections)
    mapping = eye(F32)
    for t in reversed(range(T)):
        mapping = jnp.where(t < live, -times_t(mapping, backward[t]), mapping)
        maps[t] = mapping
    chunk[R + W :] = mapping
    mapping = -dot(eye(BF16), forward[0], (1, 1))
    for t in range(T):
        if t > 0:
            mapping = jnp.where(t < live, -times_t(mapping, forward[t]), mapping)
        states[t, R:] = mapping
    chunk[R : R + W] = mapping
    state = None
    for t in range(T):
        copies[3 + 2 * t].wait()
        copies[4 + 2 * t].wait()
        driven = dot(side[t], inverse[t], (1, 1))
        if t == 0:
            state = driven
        else:
            state = jnp.where(t < live, driven - times_t(state, forward[t]), state)
        states[t, :R] = state
    chunk[:R] = state


def group_kernel(got, out, back, before, after):
    me = near_index()
    total = got[0, : R + W]
    before[...] = jnp.concatenate([jnp.zeros((R, W), F32), eye(F32)], 0)
    mapping = got[L - 1, R + W :]
    after[...] = eye(F32)
    for j in range(1, L):
        before[...] = jnp.where(me == j, total, before[...])
        total = join(total, got[j, : R + W])
        after[...] = jnp.where(me == L - 1 - j, mapping, after[...])
        mapping = times(mapping, got[L - 1 - j, R + W :])
    out[...] = half_of(total)
    back[...] = half_of(mapping)


def source_kernel(sections, got, before, states, inverse, arrow, out):
    group = lax.axis_index("zg")
    live = live_count(sections)
    parts = [
        kept(j < group, jnp.concatenate([got[2 * j], got[2 * j + 1]], 0), R) for j in range(Q - 1)
    ]
    entry = offset_of(parts, R)
    entry = times(entry, before[R:]) + before[:R]
    moved = times(entry, jnp.concatenate([states[t, R:] for t in range(T)], 1))
    total = jnp.zeros((F, W), F32)
    pad = jnp.zeros((W - R, W), BF16)
    for t in range(T):
        state = jnp.where(t < live, states[t, :R] + moved[:, t * W : (t + 1) * W], 0.0)
        high, low = split(state)
        total += dot(arrow[t], jnp.concatenate([high, pad], 0), (1, 1))
        rows = jnp.concatenate([high, low, arrow[t], jnp.zeros((F, W), BF16)], 0)
        terms = dot(rows, inverse[t], (1, 0))
        for n in range(N):
            cols = slice(n * W, (n + 1) * W)
            out[n, t * G : t * G + R] = terms[:R, cols] + terms[R : 2 * R, cols]
            out[n, t * G + R : (t + 1) * G] = terms[2 * R : 2 * R + F, cols]
    for n in range(N):
        out[n, T * G :] = total


def arrive_kernel(sections, got, backward, sums, chunk):
    live = live_count(sections)
    whole = got[0]
    for n in range(1, N):
        whole = whole + got[n]
    state = jnp.zeros((G, W), F32)
    for t in reversed(range(T)):
        source = whole[t * G : (t + 1) * G]
        state = jnp.where(t < live, source - times_t(state, backward[t]), state)
        sums[t] = state
    chunk[:G] = state
    chunk[G:] = whole[T * G :]


def back_group_kernel(got, maps, mapping, out, after):
    me = near_index()
    total = got[L - 1, :G]
    after[...] = jnp.zeros((G, W), F32)
    for j in reversed(range(L - 1)):
        after[...] = jnp.where(me == j, total, after[...])
        total = times(total, maps[j, R + W :]) + got[j, :G]
    whole = ((got[0, G:] + got[1, G:]) + got[2, G:]) + got[3, G:]
    out[:EDGE] = half_of(jnp.concatenate([total, whole], 0))
    out[EDGE:] = mapping[...]


def final_kernel(
    sections, got, after, after_map, sums, maps, side, tip_inverse, out, tip_out
):
    group = lax.axis_index("zg")
    live = live_count(sections)
    whole = got[1, EDGE - F : EDGE]
    for j in range(1, Q):
        whole = whole + got[2 * j + 1, EDGE - F : EDGE]
    gap = side[...] - whole[:, :R]
    tip = lax.dot_general(
        tip_inverse[...], gap, (((1,), (0,)), ((), ())), precision=HI, preferred_element_type=F32
    )
    tip = lax.dot_general(
        tip_inverse[...], tip, (((0,), (0,)), ((), ())), precision=HI, preferred_element_type=F32
    )
    tip_out[...] = tip

    parts = []
    for j in reversed(range(1, Q)):
        first, second = got[2 * j], got[2 * j + 1]
        part = [first[:EDGE], second[: EDGE - F], first[EDGE:], second[EDGE:]]
        parts.append(kept(j > group, jnp.concatenate(part, 0), G))
    entry = offset_of(parts, G)
    entry = times(entry, after_map[...]) + after[...]
    state = times(entry, jnp.concatenate([maps[t] for t in range(T)], 1))
    state = state + jnp.concatenate([sums[t] for t in range(T)], 1)
    tip_high, tip_low = split(tip)
    weights = jnp.concatenate(
        [tip_high.astype(F32), tip_low.astype(F32), tip_high.astype(F32)], 0
    ).astype(BF16)
    high, low = split(state[R:])
    fixed = jnp.concatenate([high.astype(F32), high.astype(F32), low.astype(F32)], 0).astype(BF16)
    state = state[:R] - dot(weights, fixed, (0, 0))
    for t in range(T):
        out[t] = jnp.where(t < live, state[:, t * W : (t + 1) * W], 0.0)


VMEM = pl.BlockSpec(memory_space=pltpu.VMEM)
SMEM = pl.BlockSpec(memory_space=pltpu.SMEM)
HBM = pl.BlockSpec(memory_space=pltpu.HBM)


def call(kernel, shapes, *args, own_copies=False, scratch=()):
    specs = [HBM if own_copies else SMEM if a.dtype == jnp.int32 else VMEM for a in args]
    shapes = [s if hasattr(s, "dtype") else jax.ShapeDtypeStruct(s, F32) for s in shapes]
    if own_copies:
        args = [pltpu.with_memory_space_constraint(a, pltpu.HBM) for a in args]
    return pl.pallas_call(
        kernel,
        out_shape=shapes,
        in_specs=specs,
        out_specs=[VMEM] * len(shapes),
        scratch_shapes=scratch,
        compiler_params=pltpu.CompilerParams(vmem_limit_bytes=16 << 20),
        name=kernel.__name__,
    )(*args)


def on_device(
    sections, right_side, tip_side, diag_inverse, forward_coupling, backward_coupling, arrow_rows, tip_inverse
):
    kept_inputs = [jax.ShapeDtypeStruct(a.shape, BF16) for a in (diag_inverse, backward_coupling)]
    states, maps, chunk, inverse, backward = call(
        local_kernel,
        [(T, R + W, W), (T, W, W), (R + 2 * W, W)] + kept_inputs,
        sections,
        right_side,
        diag_inverse,
        forward_coupling,
        backward_coupling,
        own_copies=True,
        scratch=(
            pltpu.SMEM(sections.shape, jnp.int32),
            pltpu.VMEM(right_side.shape, BF16),
            pltpu.VMEM(forward_coupling.shape, BF16),
            pltpu.SemaphoreType.DMA((3 + 2 * T,)),
        ),
    )
    near = lax.all_gather(chunk, NEAR)
    out, back, before, after_map = call(
        group_kernel, [((R + W) // 2, W), (W // 2, W), (R + W, W), (W, W)], near
    )
    got = lax.all_gather(out, FAR)
    (out,) = call(
        source_kernel,
        [(N, T * G + F, W)],
        sections,
        got,
        before,
        states,
        inverse,
        arrow_rows,
    )
    got = lax.all_to_all(out, SPACE, 0, 0, tiled=True)
    sums, chunk = call(arrive_kernel, [(T, G, W), (G + F, W)], sections, got, backward)
    got = lax.all_gather(chunk, NEAR)
    out, after = call(back_group_kernel, [(EDGE + W // 2, W), (G, W)], got, near, back)
    got = lax.all_gather(out, FAR)
    solved, tip = call(
        final_kernel,
        [(T, R, W), (F, R)],
        sections,
        got,
        after,
        after_map,
        sums,
        maps,
        tip_side.T,
        tip_inverse,
    )
    return solved, tip.T


def solution(mesh):
    torus = Mesh(mesh.devices.reshape(Q, 2, 2, 4, 4), TM + SPACE)
    return jax.shard_map(
        on_device,
        mesh=torus,
        in_specs=(
            P(),
            P(TM, None, None),
            P(),
            P(TM, SPACE, None),
            P(TM, SPACE, None),
            P(TM, SPACE, None),
            P(TM, None, SPACE),
            P(),
        ),
        out_specs=(P(TM, None, SPACE), P()),
        check_vma=False,
    )
```

```python
import functools

import jax
import jax.numpy as jnp
from jax import lax
from jax.experimental import pallas as pl
from jax.experimental.pallas import tpu as pltpu
from jax.sharding import Mesh
from jax.sharding import PartitionSpec as P

F32 = jnp.float32
BF16 = jnp.bfloat16
TM = ("zg", "zp", "core")
SPACE = ("x", "y")
NEAR = ("zp", "core")
FAR = ("zg", "core")
T = 4
R = 64
F = 8
W = 128
N = 16
G = R + F
L = 4
K = 4
PLANE = ("core",) + SPACE
Q = 8
EDGE = (G + F) // 2
HI = lax.Precision.HIGHEST


def split(x):
    high = x.astype(BF16)
    return high, (x - high.astype(F32)).astype(BF16)


def dot(a, b, dims):
    return lax.dot_general(a, b, ((dims[:1], dims[1:]), ((), ())), preferred_element_type=F32)


def times(x, m):
    xh, xl = split(x)
    mh, ml = split(m)
    return dot(jnp.concatenate([xh, xl, xh], 1), jnp.concatenate([mh, mh, ml], 0), (1, 0))


def times_t(x, c):
    xh, xl = split(x)
    return dot(jnp.concatenate([xh, xl], 1), jnp.concatenate([c, c], 1), (1, 1))


def eye(dtype):
    rows = lax.broadcasted_iota(jnp.int32, (W, W), 0)
    cols = lax.broadcasted_iota(jnp.int32, (W, W), 1)
    return jnp.where(rows == cols, 1.0, 0.0).astype(dtype)


def near_index():
    return lax.axis_index("zp") * 2 + lax.axis_index("core")


def live_count(sections):
    return sections[lax.axis_index("zg") * L + near_index()]


def join(first, then, rows=R):
    out = times(first, then[rows:])
    return jnp.concatenate([out[:rows] + then[:rows], out[rows:]], 0)


def offset_of(parts, rows):
    ahead = times(parts[0][:rows], parts[1][rows:]) + parts[1][:rows]
    middle = join(parts[2], parts[3], rows)
    behind = join(join(parts[4], parts[5], rows), parts[6], rows)
    ahead = times(ahead, middle[rows:]) + middle[:rows]
    return times(ahead, behind[rows:]) + behind[:rows]


def kept(flag, part, rows):
    neutral = jnp.concatenate([jnp.zeros((rows, W), F32), eye(F32)], 0)
    return jnp.where(flag, part, neutral)


def half_of(x):
    rows = x.shape[0] // 2
    return jnp.where(lax.axis_index("core") == 0, x[:rows], x[rows:])


def local_kernel(
    sections_in,
    side_in,
    inverse_in,
    forward_in,
    backward_in,
    states,
    maps,
    chunk,
    inverse,
    backward,
    sections,
    side,
    forward,
    sems,
):
    copies = [
        pltpu.make_async_copy(sections_in, sections, sems.at[0]),
        pltpu.make_async_copy(backward_in, backward, sems.at[1]),
        pltpu.make_async_copy(forward_in, forward, sems.at[2]),
    ]
    for t in range(T):
        copies.append(pltpu.make_async_copy(side_in.at[t], side.at[t], sems.at[3 + 2 * t]))
        copies.append(pltpu.make_async_copy(inverse_in.at[t], inverse.at[t], sems.at[4 + 2 * t]))
    for copy in copies:
        copy.start()
    for copy in copies[:3]:
        copy.wait()
    live = live_count(sections)
    mapping = eye(F32)
    for t in reversed(range(T)):
        mapping = jnp.where(t < live, -times_t(mapping, backward[t]), mapping)
        maps[t] = mapping
    chunk[R + W :] = mapping
    mapping = -dot(eye(BF16), forward[0], (1, 1))
    for t in range(T):
        if t > 0:
            mapping = jnp.where(t < live, -times_t(mapping, forward[t]), mapping)
        states[t, R:] = mapping
    chunk[R : R + W] = mapping
    state = None
    for t in range(T):
        copies[3 + 2 * t].wait()
        copies[4 + 2 * t].wait()
        driven = dot(side[t], inverse[t], (1, 1))
        if t == 0:
            state = driven
        else:
            state = jnp.where(t < live, driven - times_t(state, forward[t]), state)
        states[t, :R] = state
    chunk[:R] = state


def group_kernel(got, out, back, before, after):
    me = near_index()
    total = got[0, : R + W]
    before[...] = jnp.concatenate([jnp.zeros((R, W), F32), eye(F32)], 0)
    mapping = got[L - 1, R + W :]
    after[...] = eye(F32)
    for j in range(1, L):
        before[...] = jnp.where(me == j, total, before[...])
        total = join(total, got[j, : R + W])
        after[...] = jnp.where(me == L - 1 - j, mapping, after[...])
        mapping = times(mapping, got[L - 1 - j, R + W :])
    out[...] = half_of(total)
    back[...] = half_of(mapping)


def source_kernel(sections, got, before, states, inverse, arrow, out):
    group = lax.axis_index("zg")
    core = lax.axis_index("core")
    live = live_count(sections)
    parts = [
        kept(j < group, jnp.concatenate([got[2 * j], got[2 * j + 1]], 0), R) for j in range(Q - 1)
    ]
    entry = offset_of(parts, R)
    entry = times(entry, before[R:]) + before[:R]
    moved = times(entry, jnp.concatenate([states[t, R:] for t in range(T)], 1))
    total = jnp.zeros((F, W), F32)
    pad = jnp.zeros((W - R, W), BF16)
    for t in range(T):
        state = jnp.where(t < live, states[t, :R] + moved[:, t * W : (t + 1) * W], 0.0)
        high, low = split(state)
        total += dot(arrow[t], jnp.concatenate([high, pad], 0), (1, 1))
        rows = jnp.concatenate([high, low, arrow[t], jnp.zeros((F, W), BF16)], 0)
        terms = dot(rows, inverse[t], (1, 0))
        for n in range(N):
            cols = slice(n * W, (n + 1) * W)
            slot = jnp.where(core == 0, n, n % K * K + n // K)
            out[slot, t * G : t * G + R] = terms[:R, cols] + terms[R : 2 * R, cols]
            out[slot, t * G + R : (t + 1) * G] = terms[2 * R : 2 * R + F, cols]
    for n in range(N):
        out[n, T * G :] = total


def fold_kernel(got, out):
    for n in range(K):
        out[n] = (got[n] + got[K + n]) + (got[2 * K + n] + got[3 * K + n])


def arrive_kernel(sections, got, backward, sums, chunk):
    live = live_count(sections)
    whole = (got[0] + got[1]) + (got[2] + got[3])
    state = jnp.zeros((G, W), F32)
    for t in reversed(range(T)):
        source = whole[t * G : (t + 1) * G]
        state = jnp.where(t < live, source - times_t(state, backward[t]), state)
        sums[t] = state
    chunk[:G] = state
    chunk[G:] = whole[T * G :]


def back_group_kernel(got, maps, mapping, out, after):
    me = near_index()
    total = got[L - 1, :G]
    after[...] = jnp.zeros((G, W), F32)
    for j in reversed(range(L - 1)):
        after[...] = jnp.where(me == j, total, after[...])
        total = times(total, maps[j, R + W :]) + got[j, :G]
    whole = ((got[0, G:] + got[1, G:]) + got[2, G:]) + got[3, G:]
    out[:EDGE] = half_of(jnp.concatenate([total, whole], 0))
    out[EDGE:] = mapping[...]


def final_kernel(
    sections, got, after, after_map, sums, maps, side, tip_inverse, out, tip_out
):
    group = lax.axis_index("zg")
    live = live_count(sections)
    whole = got[1, EDGE - F : EDGE]
    for j in range(1, Q):
        whole = whole + got[2 * j + 1, EDGE - F : EDGE]
    gap = side[...] - whole[:, :R]
    tip = lax.dot_general(
        tip_inverse[...], gap, (((1,), (0,)), ((), ())), precision=HI, preferred_element_type=F32
    )
    tip = lax.dot_general(
        tip_inverse[...], tip, (((0,), (0,)), ((), ())), precision=HI, preferred_element_type=F32
    )
    tip_out[...] = tip

    parts = []
    for j in reversed(range(1, Q)):
        first, second = got[2 * j], got[2 * j + 1]
        part = [first[:EDGE], second[: EDGE - F], first[EDGE:], second[EDGE:]]
        parts.append(kept(j > group, jnp.concatenate(part, 0), G))
    entry = offset_of(parts, G)
    entry = times(entry, after_map[...]) + after[...]
    state = times(entry, jnp.concatenate([maps[t] for t in range(T)], 1))
    state = state + jnp.concatenate([sums[t] for t in range(T)], 1)
    tip_high, tip_low = split(tip)
    weights = jnp.concatenate(
        [tip_high.astype(F32), tip_low.astype(F32), tip_high.astype(F32)], 0
    ).astype(BF16)
    high, low = split(state[R:])
    fixed = jnp.concatenate([high.astype(F32), high.astype(F32), low.astype(F32)], 0).astype(BF16)
    state = state[:R] - dot(weights, fixed, (0, 0))
    for t in range(T):
        out[t] = jnp.where(t < live, state[:, t * W : (t + 1) * W], 0.0)


VMEM = pl.BlockSpec(memory_space=pltpu.VMEM)
SMEM = pl.BlockSpec(memory_space=pltpu.SMEM)
HBM = pl.BlockSpec(memory_space=pltpu.HBM)


def call(kernel, shapes, *args, own_copies=False, scratch=()):
    specs = [HBM if own_copies else SMEM if a.dtype == jnp.int32 else VMEM for a in args]
    shapes = [s if hasattr(s, "dtype") else jax.ShapeDtypeStruct(s, F32) for s in shapes]
    if own_copies:
        args = [pltpu.with_memory_space_constraint(a, pltpu.HBM) for a in args]
    return pl.pallas_call(
        kernel,
        out_shape=shapes,
        in_specs=specs,
        out_specs=[VMEM] * len(shapes),
        scratch_shapes=scratch,
        compiler_params=pltpu.CompilerParams(vmem_limit_bytes=16 << 20),
        name=kernel.__name__,
    )(*args)


def along(stage):
    groups = []
    for core in range(2):
        for line in range(K):
            steps = [k * K + line if core == stage else line * K + k for k in range(K)]
            groups.append([core * N + step for step in steps])
    return groups


def on_device(
    sections, right_side, tip_side, diag_inverse, forward_coupling, backward_coupling, arrow_rows, tip_inverse
):
    kept_inputs = [jax.ShapeDtypeStruct(a.shape, BF16) for a in (diag_inverse, backward_coupling)]
    states, maps, chunk, inverse, backward = call(
        local_kernel,
        [(T, R + W, W), (T, W, W), (R + 2 * W, W)] + kept_inputs,
        sections,
        right_side,
        diag_inverse,
        forward_coupling,
        backward_coupling,
        own_copies=True,
        scratch=(
            pltpu.SMEM(sections.shape, jnp.int32),
            pltpu.VMEM(right_side.shape, BF16),
            pltpu.VMEM(forward_coupling.shape, BF16),
            pltpu.SemaphoreType.DMA((3 + 2 * T,)),
        ),
    )
    near = lax.all_gather(chunk, NEAR)
    out, back, before, after_map = call(
        group_kernel, [((R + W) // 2, W), (W // 2, W), (R + W, W), (W, W)], near
    )
    got = lax.all_gather(out, FAR)
    (out,) = call(
        source_kernel,
        [(N, T * G + F, W)],
        sections,
        got,
        before,
        states,
        inverse,
        arrow_rows,
    )
    got = lax.all_to_all(out, PLANE, 0, 0, axis_index_groups=along(0), tiled=True)
    (out,) = call(fold_kernel, [(K, T * G + F, W)], got)
    got = lax.all_to_all(out, PLANE, 0, 0, axis_index_groups=along(1), tiled=True)
    sums, chunk = call(arrive_kernel, [(T, G, W), (G + F, W)], sections, got, backward)
    got = lax.all_gather(chunk, NEAR)
    out, after = call(back_group_kernel, [(EDGE + W // 2, W), (G, W)], got, near, back)
    got = lax.all_gather(out, FAR)
    solved, tip = call(
        final_kernel,
        [(T, R, W), (F, R)],
        sections,
        got,
        after,
        after_map,
        sums,
        maps,
        tip_side.T,
        tip_inverse,
    )
    return solved, tip.T


def solution(mesh):
    torus = Mesh(mesh.devices.reshape(Q, 2, 2, 4, 4), TM + SPACE)
    return jax.shard_map(
        on_device,
        mesh=torus,
        in_specs=(
            P(),
            P(TM, None, None),
            P(),
            P(TM, SPACE, None),
            P(TM, SPACE, None),
            P(TM, SPACE, None),
            P(TM, None, SPACE),
            P(),
        ),
        out_specs=(P(TM, None, SPACE), P()),
        check_vma=False,
    )
```

```python
import functools

import jax
import jax.numpy as jnp
from jax import lax
from jax.experimental import pallas as pl
from jax.experimental.pallas import tpu as pltpu
from jax.sharding import Mesh
from jax.sharding import PartitionSpec as P

F32 = jnp.float32
BF16 = jnp.bfloat16
TM = ("zg", "zp", "core")
SPACE = ("x", "y")
NEAR = ("zp", "core")
FAR = ("zg", "core")
T = 4
R = 64
F = 8
W = 128
N = 16
G = R + F
L = 4
K = 4
PLANE = ("core",) + SPACE
Q = 8
EDGE = (G + F) // 2
HI = lax.Precision.HIGHEST


def split(x):
    high = x.astype(BF16)
    return high, (x - high.astype(F32)).astype(BF16)


def dot(a, b, dims):
    return lax.dot_general(a, b, ((dims[:1], dims[1:]), ((), ())), preferred_element_type=F32)


def times(x, m):
    xh, xl = split(x)
    mh, ml = split(m)
    return dot(jnp.concatenate([xh, xl, xh], 1), jnp.concatenate([mh, mh, ml], 0), (1, 0))


def times_t(x, c):
    xh, xl = split(x)
    return dot(jnp.concatenate([xh, xl], 1), jnp.concatenate([c, c], 1), (1, 1))


def eye(dtype):
    rows = lax.broadcasted_iota(jnp.int32, (W, W), 0)
    cols = lax.broadcasted_iota(jnp.int32, (W, W), 1)
    return jnp.where(rows == cols, 1.0, 0.0).astype(dtype)


def near_index():
    return lax.axis_index("zp") * 2 + lax.axis_index("core")


def live_count(sections):
    return sections[lax.axis_index("zg") * L + near_index()]


def join(first, then, rows=R):
    out = times(first, then[rows:])
    return jnp.concatenate([out[:rows] + then[:rows], out[rows:]], 0)


def offset_of(parts, rows):
    ahead = times(parts[0][:rows], parts[1][rows:]) + parts[1][:rows]
    middle = join(parts[2], parts[3], rows)
    behind = join(join(parts[4], parts[5], rows), parts[6], rows)
    ahead = times(ahead, middle[rows:]) + middle[:rows]
    return times(ahead, behind[rows:]) + behind[:rows]


def kept(flag, part, rows):
    neutral = jnp.concatenate([jnp.zeros((rows, W), F32), eye(F32)], 0)
    return jnp.where(flag, part, neutral)


def half_of(x):
    rows = x.shape[0] // 2
    return jnp.where(lax.axis_index("core") == 0, x[:rows], x[rows:])


def local_kernel(
    sections_in,
    side_in,
    inverse_in,
    forward_in,
    backward_in,
    states,
    maps,
    chunk,
    counts,
    inverse,
    backward,
    sections,
    side,
    forward,
    sems,
):
    copies = [
        pltpu.make_async_copy(sections_in, sections, sems.at[0]),
        pltpu.make_async_copy(backward_in, backward, sems.at[1]),
        pltpu.make_async_copy(forward_in, forward, sems.at[2]),
    ]
    for t in range(T):
        copies.append(pltpu.make_async_copy(side_in.at[t], side.at[t], sems.at[3 + 2 * t]))
        copies.append(pltpu.make_async_copy(inverse_in.at[t], inverse.at[t], sems.at[4 + 2 * t]))
    for copy in copies:
        copy.start()
    for copy in copies[:3]:
        copy.wait()
    live = live_count(sections)
    counts[...] = jnp.full((F, W), live, jnp.int32).astype(F32)
    mapping = eye(F32)
    for t in reversed(range(T)):
        mapping = jnp.where(t < live, -times_t(mapping, backward[t]), mapping)
        maps[t] = mapping
    chunk[R + W :] = mapping
    mapping = -dot(eye(BF16), forward[0], (1, 1))
    for t in range(T):
        if t > 0:
            mapping = jnp.where(t < live, -times_t(mapping, forward[t]), mapping)
        states[t, R:] = mapping
    chunk[R : R + W] = mapping
    state = None
    for t in range(T):
        copies[3 + 2 * t].wait()
        copies[4 + 2 * t].wait()
        driven = dot(side[t], inverse[t], (1, 1))
        if t == 0:
            state = driven
        else:
            state = jnp.where(t < live, driven - times_t(state, forward[t]), state)
        states[t, :R] = state
    chunk[:R] = state


def group_kernel(got, out, back, before, after):
    me = near_index()
    total = got[0, : R + W]
    before[...] = jnp.concatenate([jnp.zeros((R, W), F32), eye(F32)], 0)
    mapping = got[L - 1, R + W :]
    after[...] = eye(F32)
    for j in range(1, L):
        before[...] = jnp.where(me == j, total, before[...])
        total = join(total, got[j, : R + W])
        after[...] = jnp.where(me == L - 1 - j, mapping, after[...])
        mapping = times(mapping, got[L - 1 - j, R + W :])
    out[...] = half_of(total)
    back[...] = half_of(mapping)


def source_kernel(counts, got, before, states, inverse, arrow, out):
    group = lax.axis_index("zg")
    core = lax.axis_index("core")
    live = counts[:1]
    parts = [
        kept(j < group, jnp.concatenate([got[2 * j], got[2 * j + 1]], 0), R) for j in range(Q - 1)
    ]
    entry = offset_of(parts, R)
    entry = times(entry, before[R:]) + before[:R]
    moved = times(entry, jnp.concatenate([states[t, R:] for t in range(T)], 1))
    total = jnp.zeros((F, W), F32)
    pad = jnp.zeros((W - R, W), BF16)
    for t in range(T):
        state = jnp.where(float(t) < live, states[t, :R] + moved[:, t * W : (t + 1) * W], 0.0)
        high, low = split(state)
        total += dot(arrow[t], jnp.concatenate([high, pad], 0), (1, 1))
        rows = jnp.concatenate([high, low, arrow[t], jnp.zeros((F, W), BF16)], 0)
        terms = dot(rows, inverse[t], (1, 0))
        for n in range(N):
            cols = slice(n * W, (n + 1) * W)
            slot = jnp.where(core == 0, n, n % K * K + n // K)
            out[slot, t * G : t * G + R] = terms[:R, cols] + terms[R : 2 * R, cols]
            out[slot, t * G + R : (t + 1) * G] = terms[2 * R : 2 * R + F, cols]
    for n in range(N):
        out[n, T * G :] = total


def fold_kernel(got, out):
    for n in range(K):
        out[n] = (got[n] + got[K + n]) + (got[2 * K + n] + got[3 * K + n])


def arrive_kernel(counts, got, backward, sums, chunk):
    live = counts[:1]
    whole = (got[0] + got[1]) + (got[2] + got[3])
    state = jnp.zeros((G, W), F32)
    for t in reversed(range(T)):
        source = whole[t * G : (t + 1) * G]
        state = jnp.where(float(t) < live, source - times_t(state, backward[t]), state)
        sums[t] = state
    chunk[:G] = state
    chunk[G:] = whole[T * G :]


def back_group_kernel(got, maps, mapping, out, after):
    me = near_index()
    total = got[L - 1, :G]
    after[...] = jnp.zeros((G, W), F32)
    for j in reversed(range(L - 1)):
        after[...] = jnp.where(me == j, total, after[...])
        total = times(total, maps[j, R + W :]) + got[j, :G]
    whole = ((got[0, G:] + got[1, G:]) + got[2, G:]) + got[3, G:]
    out[:EDGE] = half_of(jnp.concatenate([total, whole], 0))
    out[EDGE:] = mapping[...]


def final_kernel(
    counts,
    got,
    after,
    after_map,
    sums,
    maps,
    side,
    tip_inverse,
    out_final,
    tip_final,
    out,
    tip_out,
    sems,
):
    group = lax.axis_index("zg")
    live = counts[:1]
    whole = got[1, EDGE - F : EDGE]
    for j in range(1, Q):
        whole = whole + got[2 * j + 1, EDGE - F : EDGE]
    gap = side[...] - whole[:, :R]
    tip = lax.dot_general(
        tip_inverse[...], gap, (((1,), (0,)), ((), ())), precision=HI, preferred_element_type=F32
    )
    tip = lax.dot_general(
        tip_inverse[...], tip, (((0,), (0,)), ((), ())), precision=HI, preferred_element_type=F32
    )
    tip_out[...] = tip
    copies = [pltpu.make_async_copy(tip_out, tip_final, sems.at[T])]
    copies[0].start()

    parts = []
    for j in reversed(range(1, Q)):
        first, second = got[2 * j], got[2 * j + 1]
        part = [first[:EDGE], second[: EDGE - F], first[EDGE:], second[EDGE:]]
        parts.append(kept(j > group, jnp.concatenate(part, 0), G))
    entry = offset_of(parts, G)
    entry = times(entry, after_map[...]) + after[...]
    state = times(entry, jnp.concatenate([maps[t] for t in range(T)], 1))
    state = state + jnp.concatenate([sums[t] for t in range(T)], 1)
    tip_high, tip_low = split(tip)
    weights = jnp.concatenate(
        [tip_high.astype(F32), tip_low.astype(F32), tip_high.astype(F32)], 0
    ).astype(BF16)
    high, low = split(state[R:])
    fixed = jnp.concatenate([high.astype(F32), high.astype(F32), low.astype(F32)], 0).astype(BF16)
    state = state[:R] - dot(weights, fixed, (0, 0))
    for t in range(T):
        out[t] = jnp.where(float(t) < live, state[:, t * W : (t + 1) * W], 0.0)
        copies.append(pltpu.make_async_copy(out.at[t], out_final.at[t], sems.at[t]))
        copies[-1].start()
    for copy in copies:
        copy.wait()


VMEM = pl.BlockSpec(memory_space=pltpu.VMEM)
SMEM = pl.BlockSpec(memory_space=pltpu.SMEM)
HBM = pl.BlockSpec(memory_space=pltpu.HBM)


def call(kernel, shapes, *args, own_copies=False, scratch=(), outputs=None):
    specs = [HBM if own_copies else SMEM if a.dtype == jnp.int32 else VMEM for a in args]
    shapes = [s if hasattr(s, "dtype") else jax.ShapeDtypeStruct(s, F32) for s in shapes]
    if own_copies:
        args = [pltpu.with_memory_space_constraint(a, pltpu.HBM) for a in args]
    return pl.pallas_call(
        kernel,
        out_shape=shapes,
        in_specs=specs,
        out_specs=[outputs or VMEM] * len(shapes),
        scratch_shapes=scratch,
        compiler_params=pltpu.CompilerParams(vmem_limit_bytes=16 << 20),
        name=kernel.__name__,
    )(*args)


def along(stage):
    groups = []
    for core in range(2):
        for line in range(K):
            steps = [k * K + line if core == stage else line * K + k for k in range(K)]
            groups.append([core * N + step for step in steps])
    return groups


def on_device(
    sections, right_side, tip_side, diag_inverse, forward_coupling, backward_coupling, arrow_rows, tip_inverse
):
    kept_inputs = [jax.ShapeDtypeStruct(a.shape, BF16) for a in (diag_inverse, backward_coupling)]
    states, maps, chunk, counts, inverse, backward = call(
        local_kernel,
        [(T, R + W, W), (T, W, W), (R + 2 * W, W), (F, W)] + kept_inputs,
        sections,
        right_side,
        diag_inverse,
        forward_coupling,
        backward_coupling,
        own_copies=True,
        scratch=(
            pltpu.SMEM(sections.shape, jnp.int32),
            pltpu.VMEM(right_side.shape, BF16),
            pltpu.VMEM(forward_coupling.shape, BF16),
            pltpu.SemaphoreType.DMA((3 + 2 * T,)),
        ),
    )
    near = lax.all_gather(chunk, NEAR)
    out, back, before, after_map = call(
        group_kernel, [((R + W) // 2, W), (W // 2, W), (R + W, W), (W, W)], near
    )
    got = lax.all_gather(out, FAR)
    (out,) = call(
        source_kernel,
        [(N, T * G + F, W)],
        counts,
        got,
        before,
        states,
        inverse,
        arrow_rows,
    )
    got = lax.all_to_all(out, PLANE, 0, 0, axis_index_groups=along(0), tiled=True)
    (out,) = call(fold_kernel, [(K, T * G + F, W)], got)
    got = lax.all_to_all(out, PLANE, 0, 0, axis_index_groups=along(1), tiled=True)
    sums, chunk = call(arrive_kernel, [(T, G, W), (G + F, W)], counts, got, backward)
    got = lax.all_gather(chunk, NEAR)
    out, after = call(back_group_kernel, [(EDGE + W // 2, W), (G, W)], got, near, back)
    got = lax.all_gather(out, FAR)
    solved, tip = call(
        final_kernel,
        [(T, R, W), (F, R)],
        counts,
        got,
        after,
        after_map,
        sums,
        maps,
        tip_side.T,
        tip_inverse,
        outputs=HBM,
        scratch=(
            pltpu.VMEM((T, R, W), F32),
            pltpu.VMEM((F, R), F32),
            pltpu.SemaphoreType.DMA((T + 1,)),
        ),
    )
    return solved, tip.T


def solution(mesh):
    torus = Mesh(mesh.devices.reshape(Q, 2, 2, 4, 4), TM + SPACE)
    return jax.shard_map(
        on_device,
        mesh=torus,
        in_specs=(
            P(),
            P(TM, None, None),
            P(),
            P(TM, SPACE, None),
            P(TM, SPACE, None),
            P(TM, SPACE, None),
            P(TM, None, SPACE),
            P(),
        ),
        out_specs=(P(TM, None, SPACE), P()),
        check_vma=False,
    )
```

```python
import functools

import jax
import jax.numpy as jnp
from jax import lax
from jax.experimental import pallas as pl
from jax.experimental.pallas import tpu as pltpu
from jax.sharding import Mesh
from jax.sharding import PartitionSpec as P

F32 = jnp.float32
BF16 = jnp.bfloat16
TM = ("zg", "zp", "core")
SPACE = ("x", "y")
NEAR = ("zp", "core")
FAR = ("zg", "core")
T = 4
R = 64
F = 8
W = 128
N = 16
G = R + F
L = 4
K = 4
PLANE = ("core",) + SPACE
Q = 8
EDGE = (G + F) // 2
HI = lax.Precision.HIGHEST


def split(x):
    high = x.astype(BF16)
    return high, (x - high.astype(F32)).astype(BF16)


def dot(a, b, dims):
    return lax.dot_general(a, b, ((dims[:1], dims[1:]), ((), ())), preferred_element_type=F32)


def times(x, m):
    xh, xl = split(x)
    mh, ml = split(m)
    return dot(jnp.concatenate([xh, xl, xh], 1), jnp.concatenate([mh, mh, ml], 0), (1, 0))


def times_t(x, c):
    xh, xl = split(x)
    return dot(jnp.concatenate([xh, xl], 1), jnp.concatenate([c, c], 1), (1, 1))


def eye(dtype):
    rows = lax.broadcasted_iota(jnp.int32, (W, W), 0)
    cols = lax.broadcasted_iota(jnp.int32, (W, W), 1)
    return jnp.where(rows == cols, 1.0, 0.0).astype(dtype)


def near_index():
    return lax.axis_index("zp") * 2 + lax.axis_index("core")


def live_count(sections):
    return sections[lax.axis_index("zg") * L + near_index()]


def join(first, then, rows=R):
    out = times(first, then[rows:])
    return jnp.concatenate([out[:rows] + then[:rows], out[rows:]], 0)


def offset_of(parts, rows):
    ahead = times(parts[0][:rows], parts[1][rows:]) + parts[1][:rows]
    middle = join(parts[2], parts[3], rows)
    behind = join(join(parts[4], parts[5], rows), parts[6], rows)
    ahead = times(ahead, middle[rows:]) + middle[:rows]
    return times(ahead, behind[rows:]) + behind[:rows]


def kept(flag, part, rows):
    neutral = jnp.concatenate([jnp.zeros((rows, W), F32), eye(F32)], 0)
    return jnp.where(flag, part, neutral)


def half_of(x):
    rows = x.shape[0] // 2
    return jnp.where(lax.axis_index("core") == 0, x[:rows], x[rows:])


def local_kernel(
    sections_in,
    side_in,
    inverse_in,
    forward_in,
    backward_in,
    states,
    maps,
    chunk,
    counts,
    inverse,
    backward,
    sections,
    side,
    forward,
    sems,
):
    copies = [
        pltpu.make_async_copy(sections_in, sections, sems.at[0]),
        pltpu.make_async_copy(backward_in, backward, sems.at[1]),
        pltpu.make_async_copy(forward_in, forward, sems.at[2]),
    ]
    for t in range(T):
        copies.append(pltpu.make_async_copy(side_in.at[t], side.at[t], sems.at[3 + 2 * t]))
        copies.append(pltpu.make_async_copy(inverse_in.at[t], inverse.at[t], sems.at[4 + 2 * t]))
    for copy in copies:
        copy.start()
    for copy in copies[:3]:
        copy.wait()
    live = live_count(sections)
    counts[...] = jnp.full((F, W), live, jnp.int32).astype(F32)
    mapping = eye(F32)
    for t in reversed(range(T)):
        mapping = jnp.where(t < live, -times_t(mapping, backward[t]), mapping)
        maps[t] = mapping
    chunk[R + W :] = mapping
    mapping = -dot(eye(BF16), forward[0], (1, 1))
    for t in range(T):
        if t > 0:
            mapping = jnp.where(t < live, -times_t(mapping, forward[t]), mapping)
        states[t, R:] = mapping
    chunk[R : R + W] = mapping
    driven = []
    for first in (0, 2):
        for copy in copies[3 + 2 * first : 7 + 2 * first]:
            copy.wait()
        driven += [dot(side[t], inverse[t], (1, 1)) for t in (first, first + 1)]
    state = driven[0]
    states[0, :R] = state
    for t in range(1, T):
        state = jnp.where(t < live, driven[t] - times_t(state, forward[t]), state)
        states[t, :R] = state
    chunk[:R] = state


def group_kernel(got, out, back, before, after):
    me = near_index()
    total = got[0, : R + W]
    before[...] = jnp.concatenate([jnp.zeros((R, W), F32), eye(F32)], 0)
    mapping = got[L - 1, R + W :]
    after[...] = eye(F32)
    for j in range(1, L):
        before[...] = jnp.where(me == j, total, before[...])
        total = join(total, got[j, : R + W])
        after[...] = jnp.where(me == L - 1 - j, mapping, after[...])
        mapping = times(mapping, got[L - 1 - j, R + W :])
    out[...] = half_of(total)
    back[...] = half_of(mapping)


def source_kernel(counts, got, before, states, inverse, arrow, out):
    group = lax.axis_index("zg")
    core = lax.axis_index("core")
    live = counts[:1]
    parts = [
        kept(j < group, jnp.concatenate([got[2 * j], got[2 * j + 1]], 0), R) for j in range(Q - 1)
    ]
    entry = offset_of(parts, R)
    entry = times(entry, before[R:]) + before[:R]
    moved = times(entry, jnp.concatenate([states[t, R:] for t in range(T)], 1))
    total = jnp.zeros((F, W), F32)
    pad = jnp.zeros((W - R, W), BF16)
    for t in range(T):
        state = jnp.where(float(t) < live, states[t, :R] + moved[:, t * W : (t + 1) * W], 0.0)
        high, low = split(state)
        total += dot(arrow[t], jnp.concatenate([high, pad], 0), (1, 1))
        rows = jnp.concatenate([high, low, arrow[t], jnp.zeros((F, W), BF16)], 0)
        terms = dot(rows, inverse[t], (1, 0))
        for n in range(N):
            cols = slice(n * W, (n + 1) * W)
            slot = jnp.where(core == 0, n, n % K * K + n // K)
            out[slot, t * G : t * G + R] = terms[:R, cols] + terms[R : 2 * R, cols]
            out[slot, t * G + R : (t + 1) * G] = terms[2 * R : 2 * R + F, cols]
    for n in range(N):
        out[n, T * G :] = total


def fold_kernel(got, out):
    for n in range(K):
        out[n] = (got[n] + got[K + n]) + (got[2 * K + n] + got[3 * K + n])


def arrive_kernel(counts, got, backward, sums, chunk):
    live = counts[:1]
    whole = (got[0] + got[1]) + (got[2] + got[3])
    state = jnp.zeros((G, W), F32)
    for t in reversed(range(T)):
        source = whole[t * G : (t + 1) * G]
        state = jnp.where(float(t) < live, source - times_t(state, backward[t]), state)
        sums[t] = state
    chunk[:G] = state
    chunk[G:] = whole[T * G :]


def back_group_kernel(got, maps, mapping, out, after):
    me = near_index()
    total = got[L - 1, :G]
    after[...] = jnp.zeros((G, W), F32)
    for j in reversed(range(L - 1)):
        after[...] = jnp.where(me == j, total, after[...])
        total = times(total, maps[j, R + W :]) + got[j, :G]
    whole = ((got[0, G:] + got[1, G:]) + got[2, G:]) + got[3, G:]
    out[:EDGE] = half_of(jnp.concatenate([total, whole], 0))
    out[EDGE:] = mapping[...]


def final_kernel(
    counts,
    got,
    after,
    after_map,
    sums,
    maps,
    side,
    tip_inverse,
    out_final,
    tip_final,
    out,
    tip_out,
    sems,
):
    group = lax.axis_index("zg")
    live = counts[:1]
    whole = got[1, EDGE - F : EDGE]
    for j in range(1, Q):
        whole = whole + got[2 * j + 1, EDGE - F : EDGE]
    gap = side[...] - whole[:, :R]
    tip = lax.dot_general(
        tip_inverse[...], gap, (((1,), (0,)), ((), ())), precision=HI, preferred_element_type=F32
    )
    tip = lax.dot_general(
        tip_inverse[...], tip, (((0,), (0,)), ((), ())), precision=HI, preferred_element_type=F32
    )
    tip_out[...] = tip
    copies = [pltpu.make_async_copy(tip_out, tip_final, sems.at[T])]
    copies[0].start()

    parts = []
    for j in reversed(range(1, Q)):
        first, second = got[2 * j], got[2 * j + 1]
        part = [first[:EDGE], second[: EDGE - F], first[EDGE:], second[EDGE:]]
        parts.append(kept(j > group, jnp.concatenate(part, 0), G))
    entry = offset_of(parts, G)
    entry = times(entry, after_map[...]) + after[...]
    state = times(entry, jnp.concatenate([maps[t] for t in range(T)], 1))
    state = state + jnp.concatenate([sums[t] for t in range(T)], 1)
    tip_high, tip_low = split(tip)
    weights = jnp.concatenate(
        [tip_high.astype(F32), tip_low.astype(F32), tip_high.astype(F32)], 0
    ).astype(BF16)
    high, low = split(state[R:])
    fixed = jnp.concatenate([high.astype(F32), high.astype(F32), low.astype(F32)], 0).astype(BF16)
    state = state[:R] - dot(weights, fixed, (0, 0))
    for t in range(T):
        out[t] = jnp.where(float(t) < live, state[:, t * W : (t + 1) * W], 0.0)
        copies.append(pltpu.make_async_copy(out.at[t], out_final.at[t], sems.at[t]))
        copies[-1].start()
    for copy in copies:
        copy.wait()


VMEM = pl.BlockSpec(memory_space=pltpu.VMEM)
SMEM = pl.BlockSpec(memory_space=pltpu.SMEM)
HBM = pl.BlockSpec(memory_space=pltpu.HBM)


def call(kernel, shapes, *args, own_copies=False, scratch=(), outputs=None):
    specs = [HBM if own_copies else SMEM if a.dtype == jnp.int32 else VMEM for a in args]
    shapes = [s if hasattr(s, "dtype") else jax.ShapeDtypeStruct(s, F32) for s in shapes]
    if own_copies:
        args = [pltpu.with_memory_space_constraint(a, pltpu.HBM) for a in args]
    return pl.pallas_call(
        kernel,
        out_shape=shapes,
        in_specs=specs,
        out_specs=[outputs or VMEM] * len(shapes),
        scratch_shapes=scratch,
        compiler_params=pltpu.CompilerParams(vmem_limit_bytes=16 << 20),
        name=kernel.__name__,
    )(*args)


def along(stage):
    groups = []
    for core in range(2):
        for line in range(K):
            steps = [k * K + line if core == stage else line * K + k for k in range(K)]
            groups.append([core * N + step for step in steps])
    return groups


def on_device(
    sections, right_side, tip_side, diag_inverse, forward_coupling, backward_coupling, arrow_rows, tip_inverse
):
    kept_inputs = [jax.ShapeDtypeStruct(a.shape, BF16) for a in (diag_inverse, backward_coupling)]
    states, maps, chunk, counts, inverse, backward = call(
        local_kernel,
        [(T, R + W, W), (T, W, W), (R + 2 * W, W), (F, W)] + kept_inputs,
        sections,
        right_side,
        diag_inverse,
        forward_coupling,
        backward_coupling,
        own_copies=True,
        scratch=(
            pltpu.SMEM(sections.shape, jnp.int32),
            pltpu.VMEM(right_side.shape, BF16),
            pltpu.VMEM(forward_coupling.shape, BF16),
            pltpu.SemaphoreType.DMA((3 + 2 * T,)),
        ),
    )
    near = lax.all_gather(chunk, NEAR)
    out, back, before, after_map = call(
        group_kernel, [((R + W) // 2, W), (W // 2, W), (R + W, W), (W, W)], near
    )
    got = lax.all_gather(out, FAR)
    (out,) = call(
        source_kernel,
        [(N, T * G + F, W)],
        counts,
        got,
        before,
        states,
        inverse,
        arrow_rows,
    )
    got = lax.all_to_all(out, PLANE, 0, 0, axis_index_groups=along(0), tiled=True)
    (out,) = call(fold_kernel, [(K, T * G + F, W)], got)
    got = lax.all_to_all(out, PLANE, 0, 0, axis_index_groups=along(1), tiled=True)
    sums, chunk = call(arrive_kernel, [(T, G, W), (G + F, W)], counts, got, backward)
    got = lax.all_gather(chunk, NEAR)
    out, after = call(back_group_kernel, [(EDGE + W // 2, W), (G, W)], got, near, back)
    got = lax.all_gather(out, FAR)
    solved, tip = call(
        final_kernel,
        [(T, R, W), (F, R)],
        counts,
        got,
        after,
        after_map,
        sums,
        maps,
        tip_side.T,
        tip_inverse,
        outputs=HBM,
        scratch=(
            pltpu.VMEM((T, R, W), F32),
            pltpu.VMEM((F, R), F32),
            pltpu.SemaphoreType.DMA((T + 1,)),
        ),
    )
    return solved, tip.T


def solution(mesh):
    torus = Mesh(mesh.devices.reshape(Q, 2, 2, 4, 4), TM + SPACE)
    return jax.shard_map(
        on_device,
        mesh=torus,
        in_specs=(
            P(),
            P(TM, None, None),
            P(),
            P(TM, SPACE, None),
            P(TM, SPACE, None),
            P(TM, SPACE, None),
            P(TM, None, SPACE),
            P(),
        ),
        out_specs=(P(TM, None, SPACE), P()),
        check_vma=False,
    )
```

```python
import functools

import jax
import jax.numpy as jnp
from jax import lax
from jax.experimental import pallas as pl
from jax.experimental.pallas import tpu as pltpu
from jax.sharding import Mesh
from jax.sharding import PartitionSpec as P

F32 = jnp.float32
BF16 = jnp.bfloat16
TM = ("zg", "zp", "core")
SPACE = ("x", "y")
NEAR = ("zp", "core")
FAR = ("zg", "core")
T = 4
R = 64
F = 8
W = 128
N = 16
G = R + F
L = 4
K = 4
PLANE = ("core",) + SPACE
Q = 8
EDGE = (G + F) // 2
HI = lax.Precision.HIGHEST


def split(x):
    high = x.astype(BF16)
    return high, (x - high.astype(F32)).astype(BF16)


def dot(a, b, dims):
    return lax.dot_general(a, b, ((dims[:1], dims[1:]), ((), ())), preferred_element_type=F32)


def times(x, m):
    xh, xl = split(x)
    mh, ml = split(m)
    return dot(jnp.concatenate([xh, xl, xh], 1), jnp.concatenate([mh, mh, ml], 0), (1, 0))


def times_t(x, c):
    xh, xl = split(x)
    return dot(jnp.concatenate([xh, xl], 1), jnp.concatenate([c, c], 1), (1, 1))


def eye(dtype):
    rows = lax.broadcasted_iota(jnp.int32, (W, W), 0)
    cols = lax.broadcasted_iota(jnp.int32, (W, W), 1)
    return jnp.where(rows == cols, 1.0, 0.0).astype(dtype)


def near_index():
    return lax.axis_index("zp") * 2 + lax.axis_index("core")


def live_count(sections):
    return sections[lax.axis_index("zg") * L + near_index()]


def times_tall(x, m):
    xh, xl = split(x)
    mh, ml = split(m)
    both = dot(jnp.concatenate([xh, xl], 0), mh, (1, 0))
    return both[: x.shape[0]] + both[x.shape[0] :] + dot(xh, ml, (1, 0))


def join(first, then):
    out = times_tall(first, then[R:])
    return jnp.concatenate([out[:R] + then[:R], out[R:]], 0)


def offset_of(parts, flags):
    ahead = jnp.where(flags[0], parts[0][0], 0.0)
    for flag, (offset, mapping) in zip(flags[1:], parts[1:]):
        ahead = jnp.where(flag, times(ahead, mapping) + offset, ahead)
    return ahead


def half_of(x):
    rows = x.shape[0] // 2
    return jnp.where(lax.axis_index("core") == 0, x[:rows], x[rows:])


def local_kernel(
    sections_in,
    side_in,
    inverse_in,
    forward_in,
    backward_in,
    states,
    maps,
    chunk,
    counts,
    inverse,
    backward,
    sections,
    side,
    forward,
    sems,
):
    copies = [
        pltpu.make_async_copy(sections_in, sections, sems.at[0]),
        pltpu.make_async_copy(backward_in, backward, sems.at[1]),
        pltpu.make_async_copy(forward_in, forward, sems.at[2]),
    ]
    for t in range(T):
        copies.append(pltpu.make_async_copy(side_in.at[t], side.at[t], sems.at[3 + 2 * t]))
        copies.append(pltpu.make_async_copy(inverse_in.at[t], inverse.at[t], sems.at[4 + 2 * t]))
    for copy in copies:
        copy.start()
    for copy in copies[:3]:
        copy.wait()
    live = live_count(sections)
    counts[...] = jnp.full((F, W), live, jnp.int32).astype(F32)
    mapping = eye(F32)
    for t in reversed(range(T)):
        mapping = jnp.where(t < live, -times_t(mapping, backward[t]), mapping)
        maps[t] = mapping
    chunk[R + W :] = mapping
    mapping = -dot(eye(BF16), forward[0], (1, 1))
    for t in range(T):
        if t > 0:
            mapping = jnp.where(t < live, -times_t(mapping, forward[t]), mapping)
        states[t, R:] = mapping
    chunk[R : R + W] = mapping
    driven = []
    for first in (0, 2):
        for copy in copies[3 + 2 * first : 7 + 2 * first]:
            copy.wait()
        driven += [dot(side[t], inverse[t], (1, 1)) for t in (first, first + 1)]
    state = driven[0]
    states[0, :R] = state
    for t in range(1, T):
        state = jnp.where(t < live, driven[t] - times_t(state, forward[t]), state)
        states[t, :R] = state
    chunk[:R] = state


def group_kernel(got, out, back, before, after):
    me = near_index()
    total = got[0, : R + W]
    before[...] = jnp.concatenate([jnp.zeros((R, W), F32), eye(F32)], 0)
    mapping = got[L - 1, R + W :]
    after[...] = eye(F32)
    for j in range(1, L):
        before[...] = jnp.where(me == j, total, before[...])
        total = join(total, got[j, : R + W])
        after[...] = jnp.where(me == L - 1 - j, mapping, after[...])
        mapping = times_tall(mapping, got[L - 1 - j, R + W :])
    out[...] = half_of(total)
    back[...] = half_of(mapping)


def source_kernel(counts, got, before, states, inverse, arrow, out):
    group = lax.axis_index("zg")
    core = lax.axis_index("core")
    live = counts[:1]
    parts = [
        (got[2 * j, :R], jnp.concatenate([got[2 * j, R:], got[2 * j + 1]], 0)) for j in range(Q - 1)
    ]
    entry = offset_of(parts, [j < group for j in range(Q - 1)])
    entry = times(entry, before[R:]) + before[:R]
    moved = times(entry, jnp.concatenate([states[t, R:] for t in range(T)], 1))
    total = jnp.zeros((F, W), F32)
    pad = jnp.zeros((W - R, W), BF16)
    for t in range(T):
        state = jnp.where(float(t) < live, states[t, :R] + moved[:, t * W : (t + 1) * W], 0.0)
        high, low = split(state)
        total += dot(arrow[t], jnp.concatenate([high, pad], 0), (1, 1))
        rows = jnp.concatenate([high, low, arrow[t], jnp.zeros((F, W), BF16)], 0)
        terms = dot(rows, inverse[t], (1, 0))
        for n in range(N):
            cols = slice(n * W, (n + 1) * W)
            slot = jnp.where(core == 0, n, n % K * K + n // K)
            out[slot, t * G : t * G + R] = terms[:R, cols] + terms[R : 2 * R, cols]
            out[slot, t * G + R : (t + 1) * G] = terms[2 * R : 2 * R + F, cols]
    for n in range(N):
        out[n, T * G :] = total


def fold_kernel(got, out):
    for n in range(K):
        out[n] = (got[n] + got[K + n]) + (got[2 * K + n] + got[3 * K + n])


def arrive_kernel(counts, got, backward, sums, chunk):
    live = counts[:1]
    whole = (got[0] + got[1]) + (got[2] + got[3])
    state = jnp.zeros((G, W), F32)
    for t in reversed(range(T)):
        source = whole[t * G : (t + 1) * G]
        state = jnp.where(float(t) < live, source - times_t(state, backward[t]), state)
        sums[t] = state
    chunk[:G] = state
    chunk[G:] = whole[T * G :]


def back_group_kernel(got, maps, mapping, out, after):
    me = near_index()
    total = got[L - 1, :G]
    after[...] = jnp.zeros((G, W), F32)
    for j in reversed(range(L - 1)):
        after[...] = jnp.where(me == j, total, after[...])
        total = times(total, maps[j, R + W :]) + got[j, :G]
    whole = ((got[0, G:] + got[1, G:]) + got[2, G:]) + got[3, G:]
    out[:EDGE] = half_of(jnp.concatenate([total, whole], 0))
    out[EDGE:] = mapping[...]


def final_kernel(
    counts,
    got,
    after,
    after_map,
    sums,
    maps,
    side,
    tip_inverse,
    out_final,
    tip_final,
    out,
    tip_out,
    sems,
):
    group = lax.axis_index("zg")
    live = counts[:1]
    whole = got[1, EDGE - F : EDGE]
    for j in range(1, Q):
        whole = whole + got[2 * j + 1, EDGE - F : EDGE]
    gap = side[...] - whole[:, :R]
    tip = lax.dot_general(
        tip_inverse[...], gap, (((1,), (0,)), ((), ())), precision=HI, preferred_element_type=F32
    )
    tip = lax.dot_general(
        tip_inverse[...], tip, (((0,), (0,)), ((), ())), precision=HI, preferred_element_type=F32
    )
    tip_out[...] = tip
    copies = [pltpu.make_async_copy(tip_out, tip_final, sems.at[T])]
    copies[0].start()

    parts = []
    for j in reversed(range(1, Q)):
        first, second = got[2 * j], got[2 * j + 1]
        offset = jnp.concatenate([first[:EDGE], second[: EDGE - F]], 0)
        parts.append((offset, jnp.concatenate([first[EDGE:], second[EDGE:]], 0)))
    entry = offset_of(parts, [j > group for j in reversed(range(1, Q))])
    entry = times(entry, after_map[...]) + after[...]
    state = times(entry, jnp.concatenate([maps[t] for t in range(T)], 1))
    state = state + jnp.concatenate([sums[t] for t in range(T)], 1)
    tip_high, tip_low = split(tip)
    weights = jnp.concatenate(
        [tip_high.astype(F32), tip_low.astype(F32), tip_high.astype(F32)], 0
    ).astype(BF16)
    high, low = split(state[R:])
    fixed = jnp.concatenate([high.astype(F32), high.astype(F32), low.astype(F32)], 0).astype(BF16)
    state = state[:R] - dot(weights, fixed, (0, 0))
    for t in range(T):
        out[t] = jnp.where(float(t) < live, state[:, t * W : (t + 1) * W], 0.0)
        copies.append(pltpu.make_async_copy(out.at[t], out_final.at[t], sems.at[t]))
        copies[-1].start()
    for copy in copies:
        copy.wait()


VMEM = pl.BlockSpec(memory_space=pltpu.VMEM)
SMEM = pl.BlockSpec(memory_space=pltpu.SMEM)
HBM = pl.BlockSpec(memory_space=pltpu.HBM)


def call(kernel, shapes, *args, own_copies=False, scratch=(), outputs=None):
    specs = [HBM if own_copies else SMEM if a.dtype == jnp.int32 else VMEM for a in args]
    shapes = [s if hasattr(s, "dtype") else jax.ShapeDtypeStruct(s, F32) for s in shapes]
    if own_copies:
        args = [pltpu.with_memory_space_constraint(a, pltpu.HBM) for a in args]
    return pl.pallas_call(
        kernel,
        out_shape=shapes,
        in_specs=specs,
        out_specs=[outputs or VMEM] * len(shapes),
        scratch_shapes=scratch,
        compiler_params=pltpu.CompilerParams(vmem_limit_bytes=16 << 20),
        name=kernel.__name__,
    )(*args)


def along(stage):
    groups = []
    for core in range(2):
        for line in range(K):
            steps = [k * K + line if core == stage else line * K + k for k in range(K)]
            groups.append([core * N + step for step in steps])
    return groups


def on_device(
    sections, right_side, tip_side, diag_inverse, forward_coupling, backward_coupling, arrow_rows, tip_inverse
):
    kept_inputs = [jax.ShapeDtypeStruct(a.shape, BF16) for a in (diag_inverse, backward_coupling)]
    states, maps, chunk, counts, inverse, backward = call(
        local_kernel,
        [(T, R + W, W), (T, W, W), (R + 2 * W, W), (F, W)] + kept_inputs,
        sections,
        right_side,
        diag_inverse,
        forward_coupling,
        backward_coupling,
        own_copies=True,
        scratch=(
            pltpu.SMEM(sections.shape, jnp.int32),
            pltpu.VMEM(right_side.shape, BF16),
            pltpu.VMEM(forward_coupling.shape, BF16),
            pltpu.SemaphoreType.DMA((3 + 2 * T,)),
        ),
    )
    near = lax.all_gather(chunk, NEAR)
    out, back, before, after_map = call(
        group_kernel, [((R + W) // 2, W), (W // 2, W), (R + W, W), (W, W)], near
    )
    got = lax.all_gather(out, FAR)
    (out,) = call(
        source_kernel,
        [(N, T * G + F, W)],
        counts,
        got,
        before,
        states,
        inverse,
        arrow_rows,
    )
    got = lax.all_to_all(out, PLANE, 0, 0, axis_index_groups=along(0), tiled=True)
    (out,) = call(fold_kernel, [(K, T * G + F, W)], got)
    got = lax.all_to_all(out, PLANE, 0, 0, axis_index_groups=along(1), tiled=True)
    sums, chunk = call(arrive_kernel, [(T, G, W), (G + F, W)], counts, got, backward)
    got = lax.all_gather(chunk, NEAR)
    out, after = call(back_group_kernel, [(EDGE + W // 2, W), (G, W)], got, near, back)
    got = lax.all_gather(out, FAR)
    solved, tip = call(
        final_kernel,
        [(T, R, W), (F, R)],
        counts,
        got,
        after,
        after_map,
        sums,
        maps,
        tip_side.T,
        tip_inverse,
        outputs=HBM,
        scratch=(
            pltpu.VMEM((T, R, W), F32),
            pltpu.VMEM((F, R), F32),
            pltpu.SemaphoreType.DMA((T + 1,)),
        ),
    )
    return solved, tip.T


def solution(mesh):
    torus = Mesh(mesh.devices.reshape(Q, 2, 2, 4, 4), TM + SPACE)
    return jax.shard_map(
        on_device,
        mesh=torus,
        in_specs=(
            P(),
            P(TM, None, None),
            P(),
            P(TM, SPACE, None),
            P(TM, SPACE, None),
            P(TM, SPACE, None),
            P(TM, None, SPACE),
            P(),
        ),
        out_specs=(P(TM, None, SPACE), P()),
        check_vma=False,
    )
```

```python
import functools

import jax
import jax.numpy as jnp
from jax import lax
from jax.experimental import pallas as pl
from jax.experimental.pallas import tpu as pltpu
from jax.sharding import Mesh
from jax.sharding import PartitionSpec as P

F32 = jnp.float32
BF16 = jnp.bfloat16
TM = ("zg", "zp", "core")
SPACE = ("x", "y")
NEAR = ("zp", "core")
FAR = ("zg", "core")
T = 4
R = 64
F = 8
W = 128
N = 16
G = R + F
L = 4
K = 4
PLANE = ("core",) + SPACE
Q = 8
EDGE = (G + F) // 2
HI = lax.Precision.HIGHEST


def split(x):
    high = x.astype(BF16)
    return high, (x - high.astype(F32)).astype(BF16)


def dot(a, b, dims):
    return lax.dot_general(a, b, ((dims[:1], dims[1:]), ((), ())), preferred_element_type=F32)


def times(x, m):
    xh, xl = split(x)
    mh, ml = split(m)
    return dot(jnp.concatenate([xh, xl, xh], 1), jnp.concatenate([mh, mh, ml], 0), (1, 0))


def times_t(x, c):
    xh, xl = split(x)
    return dot(jnp.concatenate([xh, xl], 1), jnp.concatenate([c, c], 1), (1, 1))


def eye(dtype):
    rows = lax.broadcasted_iota(jnp.int32, (W, W), 0)
    cols = lax.broadcasted_iota(jnp.int32, (W, W), 1)
    return jnp.where(rows == cols, 1.0, 0.0).astype(dtype)


def near_index():
    return lax.axis_index("zp") * 2 + lax.axis_index("core")


def live_count(sections):
    return sections[lax.axis_index("zg") * L + near_index()]


def join(first, then, rows=R):
    out = times(first, then[rows:])
    return jnp.concatenate([out[:rows] + then[:rows], out[rows:]], 0)


def offset_of(parts, rows):
    ahead = times(parts[0][:rows], parts[1][rows:]) + parts[1][:rows]
    middle = join(parts[2], parts[3], rows)
    behind = join(join(parts[4], parts[5], rows), join(parts[6], parts[7], rows), rows)
    ahead = times(ahead, middle[rows:]) + middle[:rows]
    return times(ahead, behind[rows:]) + behind[:rows]


def kept(flag, part, rows):
    neutral = jnp.concatenate([jnp.zeros((rows, W), F32), eye(F32)], 0)
    return jnp.where(flag, part, neutral)


def half_of(x):
    rows = x.shape[0] // 2
    return jnp.where(lax.axis_index("core") == 0, x[:rows], x[rows:])


def local_kernel(
    sections_in,
    side_in,
    inverse_in,
    forward_in,
    backward_in,
    states,
    maps,
    chunk,
    counts,
    inverse,
    backward,
    sections,
    side,
    forward,
    sems,
):
    copies = [
        pltpu.make_async_copy(sections_in, sections, sems.at[0]),
        pltpu.make_async_copy(backward_in, backward, sems.at[1]),
        pltpu.make_async_copy(forward_in, forward, sems.at[2]),
    ]
    for t in range(T):
        copies.append(pltpu.make_async_copy(side_in.at[t], side.at[t], sems.at[3 + 2 * t]))
        copies.append(pltpu.make_async_copy(inverse_in.at[t], inverse.at[t], sems.at[4 + 2 * t]))
    for copy in copies:
        copy.start()
    for copy in copies[:3]:
        copy.wait()
    live = live_count(sections)
    counts[...] = jnp.full((F, W), live, jnp.int32).astype(F32)
    mapping = eye(F32)
    for t in reversed(range(T)):
        mapping = jnp.where(t < live, -times_t(mapping, backward[t]), mapping)
        maps[t] = mapping
    chunk[R + W :] = mapping
    mapping = -dot(eye(BF16), forward[0], (1, 1))
    for t in range(T):
        if t > 0:
            mapping = jnp.where(t < live, -times_t(mapping, forward[t]), mapping)
        states[t, R:] = mapping
    chunk[R : R + W] = mapping
    driven = []
    for first in (0, 2):
        for copy in copies[3 + 2 * first : 7 + 2 * first]:
            copy.wait()
        driven += [dot(side[t], inverse[t], (1, 1)) for t in (first, first + 1)]
    state = driven[0]
    states[0, :R] = state
    for t in range(1, T):
        state = jnp.where(t < live, driven[t] - times_t(state, forward[t]), state)
        states[t, :R] = state
    chunk[:R] = state


def picked(choices):
    me = near_index()
    out = choices[0]
    for j in range(1, L):
        out = jnp.where(me == j, choices[j], out)
    return out


def group_kernel(got, out, back, before, after):
    parts = [got[j, : R + W] for j in range(L)]
    maps = [got[j, R + W :] for j in range(L)]
    first, second = join(parts[0], parts[1]), join(parts[2], parts[3])
    late, early = times(maps[3], maps[2]), times(maps[1], maps[0])
    neutral = jnp.concatenate([jnp.zeros((R, W), F32), eye(F32)], 0)
    before[...] = picked([neutral, parts[0], first, join(first, parts[2])])
    after[...] = picked([times(late, maps[1]), late, maps[3], eye(F32)])
    out[...] = half_of(join(first, second))
    back[...] = half_of(times(late, early))


def source_kernel(counts, got, before, states, inverse, arrow, out):
    group = lax.axis_index("zg")
    core = lax.axis_index("core")
    live = counts[:1]
    parts = [
        kept(j < group, jnp.concatenate([got[2 * j], got[2 * j + 1]], 0), R) for j in range(Q - 1)
    ]
    entry = offset_of(parts + [before[...]], R)
    moved = times(entry, jnp.concatenate([states[t, R:] for t in range(T)], 1))
    total = jnp.zeros((F, W), F32)
    pad = jnp.zeros((W - R, W), BF16)
    for t in range(T):
        state = jnp.where(float(t) < live, states[t, :R] + moved[:, t * W : (t + 1) * W], 0.0)
        high, low = split(state)
        total += dot(arrow[t], jnp.concatenate([high, pad], 0), (1, 1))
        rows = jnp.concatenate([high, low, arrow[t], jnp.zeros((F, W), BF16)], 0)
        terms = dot(rows, inverse[t], (1, 0))
        for n in range(N):
            cols = slice(n * W, (n + 1) * W)
            slot = jnp.where(core == 0, n, n % K * K + n // K)
            out[slot, t * G : t * G + R] = terms[:R, cols] + terms[R : 2 * R, cols]
            out[slot, t * G + R : (t + 1) * G] = terms[2 * R : 2 * R + F, cols]
    for n in range(N):
        out[n, T * G :] = total


def fold_kernel(got, out):
    for n in range(K):
        out[n] = (got[n] + got[K + n]) + (got[2 * K + n] + got[3 * K + n])


def arrive_kernel(counts, got, backward, sums, chunk):
    live = counts[:1]
    whole = (got[0] + got[1]) + (got[2] + got[3])
    state = jnp.zeros((G, W), F32)
    for t in reversed(range(T)):
        source = whole[t * G : (t + 1) * G]
        state = jnp.where(float(t) < live, source - times_t(state, backward[t]), state)
        sums[t] = state
    chunk[:G] = state
    chunk[G:] = whole[T * G :]


def back_group_kernel(got, maps, mapping, out, after):
    parts = [got[j, :G] for j in range(L)]
    steps = [maps[j, R + W :] for j in range(L)]
    late = times(parts[3], steps[2]) + parts[2]
    early = times(parts[1], steps[0]) + parts[0]
    total = times(late, times(steps[1], steps[0])) + early
    after[...] = picked([times(late, steps[1]) + parts[1], late, parts[3], jnp.zeros((G, W), F32)])
    whole = ((got[0, G:] + got[1, G:]) + got[2, G:]) + got[3, G:]
    out[:EDGE] = half_of(jnp.concatenate([total, whole], 0))
    out[EDGE:] = mapping[...]


def final_kernel(
    counts,
    got,
    after,
    after_map,
    sums,
    maps,
    side,
    tip_inverse,
    out_final,
    tip_final,
    out,
    tip_out,
    sems,
):
    group = lax.axis_index("zg")
    live = counts[:1]
    whole = got[1, EDGE - F : EDGE]
    for j in range(1, Q):
        whole = whole + got[2 * j + 1, EDGE - F : EDGE]
    gap = side[...] - whole[:, :R]
    tip = lax.dot_general(
        tip_inverse[...], gap, (((1,), (0,)), ((), ())), precision=HI, preferred_element_type=F32
    )
    tip = lax.dot_general(
        tip_inverse[...], tip, (((0,), (0,)), ((), ())), precision=HI, preferred_element_type=F32
    )
    tip_out[...] = tip
    copies = [pltpu.make_async_copy(tip_out, tip_final, sems.at[T])]
    copies[0].start()

    parts = []
    for j in reversed(range(1, Q)):
        first, second = got[2 * j], got[2 * j + 1]
        part = [first[:EDGE], second[: EDGE - F], first[EDGE:], second[EDGE:]]
        parts.append(kept(j > group, jnp.concatenate(part, 0), G))
    parts.append(jnp.concatenate([after[...], after_map[...]], 0))
    entry = offset_of(parts, G)
    state = times(entry, jnp.concatenate([maps[t] for t in range(T)], 1))
    state = state + jnp.concatenate([sums[t] for t in range(T)], 1)
    tip_high, tip_low = split(tip)
    weights = jnp.concatenate(
        [tip_high.astype(F32), tip_low.astype(F32), tip_high.astype(F32)], 0
    ).astype(BF16)
    high, low = split(state[R:])
    fixed = jnp.concatenate([high.astype(F32), high.astype(F32), low.astype(F32)], 0).astype(BF16)
    state = state[:R] - dot(weights, fixed, (0, 0))
    for t in range(T):
        out[t] = jnp.where(float(t) < live, state[:, t * W : (t + 1) * W], 0.0)
        copies.append(pltpu.make_async_copy(out.at[t], out_final.at[t], sems.at[t]))
        copies[-1].start()
    for copy in copies:
        copy.wait()


VMEM = pl.BlockSpec(memory_space=pltpu.VMEM)
SMEM = pl.BlockSpec(memory_space=pltpu.SMEM)
HBM = pl.BlockSpec(memory_space=pltpu.HBM)


def call(kernel, shapes, *args, own_copies=False, scratch=(), outputs=None):
    specs = [HBM if own_copies else SMEM if a.dtype == jnp.int32 else VMEM for a in args]
    shapes = [s if hasattr(s, "dtype") else jax.ShapeDtypeStruct(s, F32) for s in shapes]
    if own_copies:
        args = [pltpu.with_memory_space_constraint(a, pltpu.HBM) for a in args]
    return pl.pallas_call(
        kernel,
        out_shape=shapes,
        in_specs=specs,
        out_specs=[outputs or VMEM] * len(shapes),
        scratch_shapes=scratch,
        compiler_params=pltpu.CompilerParams(vmem_limit_bytes=16 << 20),
        name=kernel.__name__,
    )(*args)


def along(stage):
    groups = []
    for core in range(2):
        for line in range(K):
            steps = [k * K + line if core == stage else line * K + k for k in range(K)]
            groups.append([core * N + step for step in steps])
    return groups


def on_device(
    sections, right_side, tip_side, diag_inverse, forward_coupling, backward_coupling, arrow_rows, tip_inverse
):
    kept_inputs = [jax.ShapeDtypeStruct(a.shape, BF16) for a in (diag_inverse, backward_coupling)]
    states, maps, chunk, counts, inverse, backward = call(
        local_kernel,
        [(T, R + W, W), (T, W, W), (R + 2 * W, W), (F, W)] + kept_inputs,
        sections,
        right_side,
        diag_inverse,
        forward_coupling,
        backward_coupling,
        own_copies=True,
        scratch=(
            pltpu.SMEM(sections.shape, jnp.int32),
            pltpu.VMEM(right_side.shape, BF16),
            pltpu.VMEM(forward_coupling.shape, BF16),
            pltpu.SemaphoreType.DMA((3 + 2 * T,)),
        ),
    )
    near = lax.all_gather(chunk, NEAR)
    out, back, before, after_map = call(
        group_kernel, [((R + W) // 2, W), (W // 2, W), (R + W, W), (W, W)], near
    )
    got = lax.all_gather(out, FAR)
    (out,) = call(
        source_kernel,
        [(N, T * G + F, W)],
        counts,
        got,
        before,
        states,
        inverse,
        arrow_rows,
    )
    got = lax.all_to_all(out, PLANE, 0, 0, axis_index_groups=along(0), tiled=True)
    (out,) = call(fold_kernel, [(K, T * G + F, W)], got)
    got = lax.all_to_all(out, PLANE, 0, 0, axis_index_groups=along(1), tiled=True)
    sums, chunk = call(arrive_kernel, [(T, G, W), (G + F, W)], counts, got, backward)
    got = lax.all_gather(chunk, NEAR)
    out, after = call(back_group_kernel, [(EDGE + W // 2, W), (G, W)], got, near, back)
    got = lax.all_gather(out, FAR)
    solved, tip = call(
        final_kernel,
        [(T, R, W), (F, R)],
        counts,
        got,
        after,
        after_map,
        sums,
        maps,
        tip_side.T,
        tip_inverse,
        outputs=HBM,
        scratch=(
            pltpu.VMEM((T, R, W), F32),
            pltpu.VMEM((F, R), F32),
            pltpu.SemaphoreType.DMA((T + 1,)),
        ),
    )
    return solved, tip.T


def solution(mesh):
    torus = Mesh(mesh.devices.reshape(Q, 2, 2, 4, 4), TM + SPACE)
    return jax.shard_map(
        on_device,
        mesh=torus,
        in_specs=(
            P(),
            P(TM, None, None),
            P(),
            P(TM, SPACE, None),
            P(TM, SPACE, None),
            P(TM, SPACE, None),
            P(TM, None, SPACE),
            P(),
        ),
        out_specs=(P(TM, None, SPACE), P()),
        check_vma=False,
    )
```
